32 devices in a mesh: row: 4 (over x, core), col: 8 (over z, y).
Axes of the slice: x: 2, y: 2, z: 4, core: 2. Of those that a mesh axis runs over, the one named last changes fastest.
Arguments:
- w_inter: bfloat16 [3072, 4, 1024], P('col', 'row'), may hold values from -0.109375 to 0.109375
- t_panel: bfloat16 [1024, 4, 3072], P('col', None, 'row'), may hold values from -6 to 6
- amplitudes: float32 [1024, 4, 4, 1024], P('col', None, 'row'), may hold values from -4 to 4
- e_occ: float32 [4], replicated, may hold values from -2 to -0.5
- e_vir: float32 [1024], replicated, may hold values from 0.3 to 3
Outputs:
- new_amplitudes: float32 [1024, 4, 4, 1024], P('col', None, 'row')
The draws below stay inside these ranges and needn't reach their ends.
All inputs are finite; a program needn't handle non-finite values.
Results may differ from the reference program's by a relative error of at most 0.0003.
Values may be sent and summed in bfloat16 or wider, within the bound.
A program may use at most 64 MiB of HBM per device.

```python
import jax
import jax.numpy as jnp

V = 1024
KDIM = 3072
OCC = 4


def steps_of(key, extent, pieces, least, high):
    def one(position, parts):
        draws = jax.random.uniform(jax.random.fold_in(jax.random.fold_in(key, 6), position), (parts,), jnp.float32, least / len(pieces), high / len(pieces))
        return jnp.repeat(jnp.exp(draws), extent[position] // parts).reshape((-1,) + (1,) * (len(extent) - position - 1))

    factor_of = one(*pieces[0])
    for cut in pieces[1:]:
        factor_of = factor_of * one(*cut)
    return factor_of


def scatter_about(rng, shape, scale, most, cuts=(), dtype=jnp.bfloat16):
    factor_of = steps_of(rng, shape, cuts, -0.22, 0.18) if cuts else 1.0
    result = jax.random.normal(rng, shape, jnp.float32) * scale * factor_of
    return jnp.minimum(jnp.maximum(result, -most), most).astype(dtype)


def setup_inputs(seed: int = 0) -> dict:
    splits = jax.random.split(jax.random.key(seed), 6)
    w_inter = scatter_about(splits[0], (KDIM, OCC, V), KDIM ** -0.5, 0.109375, ((0, 8), (1, 4)))
    t_panel = scatter_about(splits[1], (V, OCC, KDIM), 1.0, 6.0, ((0, 8), (2, 4)))
    amplitudes = scatter_about(splits[2], (V, OCC, OCC, V), 0.5, 4.0, ((0, 8), (2, 4)), jnp.float32)
    e_occ = jnp.clip(jax.random.uniform(splits[3], (OCC,), jnp.float32, -2.0, -0.5), -2.0, -0.5)
    e_vir = jnp.clip(jax.random.uniform(splits[4], (V,), jnp.float32, 0.3, 3.0), 0.3, 3.0)
    return dict(w_inter=w_inter, t_panel=t_panel, amplitudes=amplitudes, e_occ=e_occ, e_vir=e_vir)


def reference(w_inter, t_panel, amplitudes, e_occ, e_vir):
    t_matrix = t_panel.reshape(V * OCC, KDIM)
    w_matrix = w_inter.reshape(KDIM, OCC * V)
    contracted = jnp.dot(t_matrix, w_matrix, preferred_element_type=jnp.float32).reshape(V, OCC, OCC, V)
    residual = contracted + jnp.transpose(contracted, (3, 2, 1, 0))
    gaps = (e_occ[None, :, None, None] + e_occ[None, None, :, None]
            - e_vir[:, None, None, None] - e_vir[None, None, None, :])
    return amplitudes + residual / gaps
```

```python
import functools
import math

import jax
import jax.numpy as jnp
from jax import lax
from jax.experimental import pallas as pl
from jax.experimental.pallas import tpu as pltpu
from jax.sharding import PartitionSpec as P

MESH = pl.DeviceIdType.MESH
POWER = 7
LARGEST_T = 6.0
LARGEST_W = 0.109375


def coded(x, scale):
    x = x * scale
    x2 = x * x
    return (x2 * x2 * x2 * x).astype(jnp.bfloat16)


def decoded(y, scale):
    y = y.astype(jnp.float32)
    size = jnp.abs(y)
    root = jnp.exp2(jnp.log2(jnp.maximum(size, 1e-37)) * (1.0 / POWER)) * (1.0 / scale)
    root = jnp.where(size < 1e-37, 0.0, root)
    return jnp.where(y < 0, -root, root)


def kernel(
    rows, height, scale,
    w_ref, t_ref, eo_ref, evb_ref, eva_ref, out_ref,
    w_all, w_thru, t_all, acc, enc, mirror, renc, rin,
    local_sem, w_send, w_recv, wy_send, wy_recv,
    t_send, t_recv, t_core_send, t_core_recv, m_send, m_recv, r_send, r_recv,
):
    r = lax.axis_index("row")
    c = lax.axis_index("col")
    z, y = c // 2, c % 2
    q, pair = z % 2, z // 2
    partner = z + 1 - 2 * q
    upper = jnp.where(2 * z >= height, 1, 0)
    quads = rows // 2
    core, quad = r % 2, r // 2
    core_partner = r + 1 - 2 * core
    vd = evb_ref.shape[1]
    occ = eo_ref.shape[0]
    kw = w_ref.shape[0]
    half = height * vd
    pairs = height // 4
    pair_here = pair - upper * pairs
    chunks, width = acc.shape[1], acc.shape[3]
    cuts, pieces = wy_send.shape[1], t_send.shape[2]
    grouped = width // vd

    def remote(source, target, send, recv, device):
        return pltpu.make_async_remote_copy(source, target, send, recv, device_id=device, device_id_type=MESH)

    def at_plane(pr, pz, py):
        return (pr, 2 * pz + py)

    def w_own(h, n=None):
        lane = pl.ds(pl.multiple_of(h * half, 128), half)
        if n is None:
            return w_ref.at[:, lane]
        return w_ref.at[pl.ds(n * (kw // cuts), kw // cuts), lane]

    def w_block(block, part):
        return w_all.at[block, pl.ds(pl.multiple_of(part * kw, kw), kw), :]

    def w_cut(block, part, n):
        size = kw // cuts
        return w_all.at[block, pl.ds(pl.multiple_of(part * kw + n * size, size), size), :]

    w_local = pltpu.make_async_copy(w_own(q), w_block(z, y), local_sem.at[0])
    t_local = pltpu.make_async_copy(t_ref, t_all.at[q, r], local_sem.at[1])
    w_local.start()
    t_local.start()

    barrier = pltpu.get_barrier_semaphore()

    def greet(device):
        pl.semaphore_signal(barrier, inc=1, device_id=device, device_id_type=MESH)

    def mirror_peer(n):
        pr, rest = n // (2 * pairs), n % (2 * pairs)
        return pr, 2 * (q * pairs + rest // 2) + upper, rest % 2

    def is_self(pr, pz, py):
        return jnp.logical_and(jnp.logical_and(pr == r, pz == z), py == y)

    def greet_row(d, carry):
        greet((lax.rem(r + d, rows), c))
        return carry

    def greet_mirror(n, carry):
        pr, pz, py = mirror_peer(n)

        @pl.when(jnp.logical_not(is_self(pr, pz, py)))
        def _():
            greet(at_plane(pr, pz, py))
        return carry

    @pl.when(z + 1 < height)
    def _():
        greet(at_plane(r, z + 1, y))

    @pl.when(z >= 1)
    def _():
        greet(at_plane(r, z - 1, y))

    greet(at_plane(r, z, 1 - y))
    lax.fori_loop(1, rows, greet_row, 0)
    lax.fori_loop(0, 2 * pairs * rows, greet_mirror, 0)
    lines_here = jnp.where(z + 1 < height, 1, 0) + jnp.where(z >= 1, 1, 0)
    selves = jnp.where(q == upper, 1, 0)
    pl.semaphore_wait(barrier, lines_here + rows + 2 * pairs * rows - selves)

    toward = 1 - 2 * q
    ways = (toward, -toward)

    def exists(plane):
        return jnp.logical_and(plane >= 0, plane < height)

    def sends(side, step, kind):
        way = ways[side]
        return jnp.logical_and(exists(z + way * (1 + kind)), exists(z - way * step))

    def receives(side, step, kind):
        way = ways[side]
        return jnp.logical_and(exists(z + way * (1 + step)), exists(z - way * kind))

    def came_from(side, step):
        return z + ways[side] * (1 + step)

    def rows_of(n):
        size = kw // cuts
        return pl.ds(n * size, size)

    def line_copy(side, step, kind, n, incoming=False):
        way = ways[side]
        block = came_from(side, step) if incoming else z - way * step
        near = w_cut(block, y, n)
        far = w_thru.at[block, rows_of(n), :]
        place = near if kind == 0 else far
        if incoming:
            source = place
        elif step == 0:
            source = w_own(1 - q if kind == 0 else q, n)
        else:
            source = far if kind == 0 else near
        return remote(
            source, place, w_send.at[side, step, kind, n], w_recv.at[side, step, kind, n],
            at_plane(r, z + way, y))

    def send_line(side, step, kind, n):
        if step < height - 1:
            @pl.when(sends(side, step, kind))
            def _():
                line_copy(side, step, kind, n).start()

    def across(block, n, own=False):
        return remote(
            w_own(q, n) if own else w_cut(block, y, n), w_cut(block, y, n),
            wy_send.at[block, n], wy_recv.at[block, n], at_plane(r, z, 1 - y))

    def across_in(block, n):
        return remote(
            w_cut(block, 1 - y, n), w_cut(block, 1 - y, n),
            wy_send.at[block, n], wy_recv.at[block, n], at_plane(r, z, 1 - y))

    def relay(side, step, kind, only=None):
        take = receives(side, step, kind)
        if only is not None:
            take = jnp.logical_and(take, only)

        @pl.when(take)
        def _():
            for n in range(cuts):
                line_copy(side, step, kind, n, True).wait_recv()
                if kind == 0:
                    across(came_from(side, step), n).start()
                send_line(1 - side, step + 1, 1 - kind, n)

    t_size = t_ref.shape[0] // pieces

    def t_rows(m):
        return pl.ds(m * t_size, t_size)

    def t_from(which, source_r, m):
        return t_all.at[which, source_r, t_rows(m), :]

    def t_copy(which, source_r, m, device, send, recv):
        return remote(t_from(which, source_r, m), t_from(which, source_r, m), send, recv, device)

    def t_row(k, d, m):
        which = q if k == 0 else 1 - q
        target = 2 * lax.rem(quad + d, quads) + core
        source = t_ref.at[t_rows(m), :] if k == 0 else t_from(which, r, m)
        return remote(source, t_from(which, r, m), t_send.at[k, d, m], t_recv.at[k, d, m], (target, c))

    def t_core(k, d, source_r, m):
        which = q if k == 0 else 1 - q
        source = t_ref.at[t_rows(m), :] if k == 0 and d == 0 else t_from(which, source_r, m)
        return remote(
            source, t_from(which, source_r, m), t_core_send.at[k, d, m], t_core_recv.at[k, d, m], (core_partner, c))

    def t_row_in(k, d, m):
        which = q if k == 0 else 1 - q
        source_r = 2 * lax.rem(quad + quads - d, quads) + core
        t_copy(which, source_r, m, (r, c), t_send.at[k, d, m], t_recv.at[k, d, m]).wait_recv()
        t_core(k, d, source_r, m).start()

    def t_rows_in(k, m):
        for d in range(1, quads):
            t_row_in(k, d, m)

    def t_plane(m):
        return remote(
            t_ref.at[t_rows(m), :], t_from(q, r, m), t_send.at[0, 0, m], t_recv.at[0, 0, m],
            at_plane(r, partner, y))

    def t_plane_in(m):
        t_copy(1 - q, r, m, at_plane(r, partner, y), t_send.at[0, 0, m], t_recv.at[0, 0, m]).wait_recv()
        for d in range(1, quads):
            t_row(1, d, m).start()
        t_core(1, 0, r, m).start()

    def wait_t_core(k):
        for d in range(quads):
            source_r = 2 * lax.rem(quad + quads - d, quads) + 1 - core
            for m in range(pieces):
                t_core(k, d, source_r, m).wait_recv()

    for m in range(pieces):
        for d in range(1, quads):
            t_row(0, d, m).start()
    t_plane(0).start()
    for n in range(cuts):
        across(z, n, True).start()
    for kind in range(2):
        for n in range(cuts):
            send_line(1, 0, kind, n)
    for n in range(cuts):
        send_line(0, 0, 1, n)
    at_end = jnp.logical_or(z == 0, z == height - 1)
    inside = jnp.logical_not(at_end)

    @pl.when(at_end)
    def _():
        for m in range(1, pieces - 1):
            t_plane(m).start()
        for n in range(cuts):
            send_line(0, 0, 0, n)
        t_plane(pieces - 1).start()

    @pl.when(inside)
    def _():
        for n in range(cuts):
            send_line(0, 0, 0, n)
        for m in range(1, pieces):
            t_plane(m).start()

    for m in range(pieces):
        t_core(0, 0, r, m).start()

    tile = min(256, t_ref.shape[0])
    tiles = t_ref.shape[0] // tile

    def multiply(p, block, first):
        def body(n, carry):
            at = pl.ds(pl.multiple_of(n * tile, tile), tile)
            product = jnp.dot(t_all[p, block, at, :], w_all[block], preferred_element_type=jnp.float32)
            for m in range(chunks):
                part = product[:, m * width:(m + 1) * width]
                if first:
                    acc[p, m, at, :] = part
                else:
                    acc[p, m, at, :] += part
            return carry

        lax.fori_loop(0, tiles, body, 0)

    def multiply_from(side, step, own, only=None):
        take = receives(side, step, 0)
        if only is not None:
            take = jnp.logical_and(take, only)

        @pl.when(take)
        def _():
            block = came_from(side, step)
            if own:
                for n in range(cuts):
                    across_in(block, n).wait_recv()
            multiply(q if own else 1 - q, block, False)

    def mirror_copy(g, n):
        pr, pz, py = mirror_peer(n)
        return remote(
            enc.at[g, n], mirror.at[r, pair_here, y, g],
            m_send.at[g, n], m_recv.at[r, pair_here, y, g], at_plane(pr, pz, py))

    def mirror_self(g, n):
        return pltpu.make_async_copy(enc.at[g, n], mirror.at[r, pair_here, y, g], local_sem.at[2 + g])

    def mirror_start(g):
        def send_mirror(m, carry):
            j = lax.rem(r + m + 1, occ)
            at = pl.ds(pl.multiple_of(j * vd, vd), vd)
            for place in range(chunks):
                values = coded(acc[g, place, at, :], scale)
                for b in range(grouped):
                    block = place * grouped + b
                    rest = 2 * (block // 4) + block % 2
                    enc[g, j * 2 * pairs + rest, block % 4 // 2] = values[:, b * vd:(b + 1) * vd]
            for rest in range(2 * pairs):
                n = j * 2 * pairs + rest
                pr, pz, py = mirror_peer(n)
                here = is_self(pr, pz, py)

                @pl.when(here)
                def _():
                    mirror_self(g, n).start()

                @pl.when(jnp.logical_not(here))
                def _():
                    mirror_copy(g, n).start()
            return carry

        lax.fori_loop(0, occ, send_mirror, 0)

    relay(1, 0, 0)
    for m in range(pieces // 2):
        t_rows_in(0, m)
    t_plane_in(0)
    relay(0, 0, 1)
    relay(0, 0, 0, at_end)
    for m in range(pieces // 2, pieces):
        t_rows_in(0, m)
    relay(1, 0, 1)
    t_plane_in(1)
    w_local.wait()
    t_local.wait()
    wait_t_core(0)
    for n in range(cuts):
        across_in(z, n).wait_recv()
    multiply(q, z, True)
    for m in range(2, pieces - 1):
        t_plane_in(m)
    t_rows_in(1, 0)
    multiply_from(1, 0, True)
    for step in range(1, height - 2):
        relay(1, step, 0)
        relay(0, step, 1)
        if step == 1:
            t_rows_in(1, 1)
        relay(0, step - 1, 0, inside if step == 1 else None)
        if step == 1:
            t_plane_in(pieces - 1)
            multiply_from(0, 0, True, at_end)
        multiply_from(1, step, True)
        relay(1, step, 1)
    relay(0, height - 3, 0)
    for m in range(2, pieces):
        t_rows_in(1, m)
    multiply_from(0, 0, True, inside)
    for step in range(1, height - 2):
        multiply_from(0, step, True)

    @pl.when(inside)
    def _():
        mirror_start(q)

    wait_t_core(1)
    multiply(1 - q, z, True)
    for step in range(height - 2):
        multiply_from(1, step, False)
        multiply_from(0, step, False)

    @pl.when(inside)
    def _():
        mirror_start(1 - q)

    @pl.when(at_end)
    def _():
        relay(0, height - 2, 0)
        multiply_from(0, height - 2, True)
        mirror_start(q)
        multiply_from(0, height - 2, False)
        mirror_start(1 - q)

    lanes = max(128, vd)
    lines = width // lanes
    lines_all = 2 * half // lanes
    vir_mine = jnp.broadcast_to(evb_ref[pl.ds(c, 1), :], (lanes, vd)).T

    def write(j, h, place, value):
        for n in range(lines):
            line = (h * chunks + place) * lines + n
            gaps = (eo_ref[j] + eo_ref[r]) - vir_mine - eva_ref[pl.ds(line, 1), :]
            out_ref[pl.ds(j * lines_all + line, vd, stride=occ * lines_all), :] = (
                value[:, n * lanes:(n + 1) * lanes] / gaps)

    def update_copy(place, j):
        return remote(
            renc.at[place, j], rin.at[place, j], r_send.at[place, j], r_recv.at[place, j],
            at_plane(r, partner, y))

    def finish(n, carry):
        j = lax.rem(r + n, occ)
        order = n // occ
        if grouped == 2:
            s = order % pairs
            g = lax.rem(upper + order // pairs, 2)
            place = 2 * s + g
            blocks = [(g, 0), (g, 1)]
        else:
            s = place = order
            blocks = [(0, 0), (0, 1), (1, 0), (1, 1)]
        sender = 2 * (q * pairs + s) + upper
        for g, py in blocks:
            here = is_self(j, sender, py)

            @pl.when(here)
            def _():
                mirror_self(g, j * 2 * pairs + 2 * s + py).wait()

            @pl.when(jnp.logical_not(here))
            def _():
                remote(
                    enc.at[g, 0], mirror.at[j, s, py, g], m_send.at[g, 0], m_recv.at[j, s, py, g],
                    at_plane(j, sender, py)).wait_recv()
        at = pl.ds(pl.multiple_of(j * vd, vd), vd)

        def whole(p):
            theirs = [decoded(mirror[j, s, py, g, p], scale).T for g, py in blocks]
            return acc[p, place, at, :] + jnp.concatenate(theirs, axis=1)

        renc[place, j] = coded(whole(1 - q), scale)
        update_copy(place, j).start()
        write(j, q, place, whole(q))
        return carry

    lax.fori_loop(0, chunks * occ, finish, 0)

    def last(n, carry):
        j = lax.rem(r + n, occ)
        place = lax.rem(n // occ + chunks // 2 * q, chunks)
        update_copy(place, j).wait_recv()
        write(j, 1 - q, place, decoded(rin[place, j], scale))
        return carry

    lax.fori_loop(0, chunks * occ, last, 0)

    def sent_update(n, carry):
        update_copy(n // occ, n % occ).wait_send()
        return carry

    lax.fori_loop(0, chunks * occ, sent_update, 0)

    def sent_mirror(n, carry):
        for g in range(2):
            pr, pz, py = mirror_peer(n)

            @pl.when(jnp.logical_not(is_self(pr, pz, py)))
            def _():
                mirror_copy(g, n).wait_send()
        return carry

    lax.fori_loop(0, 2 * pairs * occ, sent_mirror, 0)
    for block in range(height):
        for n in range(cuts):
            across(block, n).wait_send()
    for step in range(height - 1):
        for side in range(2):
            for kind in range(2):
                @pl.when(sends(side, step, kind))
                def _():
                    for n in range(cuts):
                        line_copy(side, step, kind, n).wait_send()
    for m in range(pieces):
        t_plane(m).wait_send()
        for k in range(2):
            for d in range(1, quads):
                t_row(k, d, m).wait_send()
            for d in range(quads):
                t_core(k, d, r, m).wait_send()


def on_device(rows, cols, w_inter, t_panel, amplitudes, e_occ, e_vir):
    kw, occ_dev, vir_all = w_inter.shape
    vd, occ, kt = t_panel.shape
    height = cols // 2
    bound = LARGEST_T * LARGEST_W * kw * cols
    scale = 2.0 ** math.floor(119.0 / POWER - math.log2(bound))
    w_matrix = w_inter.reshape(kw, vir_all)
    t_rows = jnp.transpose(t_panel, (1, 0, 2)).reshape(occ * vd, kt)
    half = vir_all // 2
    grouped = 2 if 2 * vd % 128 == 0 else 4
    width = grouped * vd
    chunks = half // width
    pairs = height // 4
    cuts = 2 if kw % 32 == 0 else 1
    pieces = 4
    dma = pltpu.SemaphoreType.DMA
    vmem = pl.BlockSpec(memory_space=pltpu.VMEM)
    lanes = max(128, vd)
    smem = pl.BlockSpec(memory_space=pltpu.SMEM)
    update = pl.pallas_call(
        functools.partial(kernel, rows, height, scale),
        out_shape=jax.ShapeDtypeStruct((vd * occ * vir_all // lanes, lanes), jnp.float32),
        in_specs=[pl.BlockSpec(memory_space=pl.ANY), vmem, smem, vmem, vmem],
        out_specs=vmem,
        scratch_shapes=[
            pltpu.VMEM((height, 2 * kw, half), jnp.bfloat16),
            pltpu.VMEM((height, kw, half), jnp.bfloat16),
            pltpu.VMEM((2, rows, occ * vd, kt), jnp.bfloat16),
            pltpu.VMEM((2, chunks, occ * vd, width), jnp.float32),
            pltpu.VMEM((2, occ * 2 * pairs, 2, vd, vd), jnp.bfloat16),
            pltpu.VMEM((rows, pairs, 2, 2, 2, vd, vd), jnp.bfloat16),
            pltpu.VMEM((chunks, occ, vd, width), jnp.bfloat16),
            pltpu.VMEM((chunks, occ, vd, width), jnp.bfloat16),
            dma((4,)),
            dma((2, height - 1, 2, cuts)),
            dma((2, height - 1, 2, cuts)),
            dma((height, cuts)),
            dma((height, cuts)),
            dma((2, rows // 2, pieces)),
            dma((2, rows // 2, pieces)),
            dma((2, rows // 2, pieces)),
            dma((2, rows // 2, pieces)),
            dma((2, occ * 2 * pairs)),
            dma((rows, pairs, 2, 2)),
            dma((chunks, occ)),
            dma((chunks, occ)),
        ],
        compiler_params=pltpu.CompilerParams(
            collective_id=0, has_side_effects=True, vmem_limit_bytes=60 * 1024 * 1024),
        name="amplitude_residual",
    )(w_matrix, t_rows, e_occ, e_vir.reshape(cols, vd), e_vir.reshape(vir_all // lanes, lanes))
    return (lax.optimization_barrier(amplitudes.reshape(update.shape)) + update).reshape(amplitudes.shape)


def solution(mesh):
    rows, cols = mesh.shape["row"], mesh.shape["col"]
    return jax.shard_map(
        functools.partial(on_device, rows, cols),
        mesh=mesh,
        in_specs=(
            P("col", "row", None),
            P("col", None, "row"),
            P("col", None, "row", None),
            P(),
            P(),
        ),
        out_specs=P("col", None, "row", None),
        check_vma=False,
    )
```

```python
import functools
import math

import jax
import jax.numpy as jnp
from jax import lax
from jax.experimental import pallas as pl
from jax.experimental.pallas import tpu as pltpu
from jax.sharding import PartitionSpec as P

MESH = pl.DeviceIdType.MESH
POWER = 7
LARGEST_T = 6.0
LARGEST_W = 0.109375


def coded(x, scale):
    x = x * scale
    x2 = x * x
    return (x2 * x2 * x2 * x).astype(jnp.bfloat16)


def decoded(y, scale):
    y = y.astype(jnp.float32)
    size = jnp.abs(y)
    root = jnp.exp2(jnp.log2(jnp.maximum(size, 1e-37)) * (1.0 / POWER)) * (1.0 / scale)
    root = jnp.where(size < 1e-37, 0.0, root)
    return jnp.where(y < 0, -root, root)


def kernel(
    rows, height, scale,
    w_ref, t_ref, eo_ref, evb_ref, eva_ref, out_ref,
    w_all, w_thru, t_all, acc, enc, mirror, renc, rin,
    local_sem, w_sem, w_send, w_recv, wy_send, wy_recv,
    t_send, t_recv, t_core_send, t_core_recv, m_send, m_recv, r_send, r_recv,
):
    r = lax.axis_index("row")
    c = lax.axis_index("col")
    z, y = c // 2, c % 2
    q, pair = z % 2, z // 2
    partner = z + 1 - 2 * q
    upper = jnp.where(2 * z >= height, 1, 0)
    quads = rows // 2
    core, quad = r % 2, r // 2
    core_partner = r + 1 - 2 * core
    vd = evb_ref.shape[1]
    occ = eo_ref.shape[0]
    kw = w_ref.shape[0]
    half = height * vd
    pairs = height // 4
    pair_here = pair - upper * pairs
    chunks, width = acc.shape[1], acc.shape[3]
    grouped = width // vd
    parts = mirror.shape[4]
    pieces = t_send.shape[2]
    many = chunks // 2

    def remote(source, target, send, recv, device):
        return pltpu.make_async_remote_copy(source, target, send, recv, device_id=device, device_id_type=MESH)

    def at_plane(pr, pz, py):
        return (pr, 2 * pz + py)

    def chunk_of(phase, n, h):
        return 2 * n + jnp.where(h == 1, phase, 1 - phase) if parts == 2 else phase * many + n

    def w_own(h, m):
        return w_ref.at[:, pl.ds(pl.multiple_of(h * half + m * width, 128), width)]

    def w_block(block, part, m):
        return w_all.at[block, m, pl.ds(pl.multiple_of(part * kw, kw), kw), :]

    def w_local(m):
        return pltpu.make_async_copy(w_own(q, m), w_block(z, y, m), w_sem.at[m])

    for m in range(chunks):
        w_local(m).start()
    t_local = pltpu.make_async_copy(t_ref, t_all.at[q, r], local_sem.at[0])
    t_local.start()

    barrier = pltpu.get_barrier_semaphore()

    def greet(device):
        pl.semaphore_signal(barrier, inc=1, device_id=device, device_id_type=MESH)

    def mirror_peer(n):
        pr, rest = n // (2 * pairs), n % (2 * pairs)
        return pr, 2 * (q * pairs + rest // 2) + upper, rest % 2

    def is_self(pr, pz, py):
        return jnp.logical_and(jnp.logical_and(pr == r, pz == z), py == y)

    def greet_row(d, carry):
        greet((lax.rem(r + d, rows), c))
        return carry

    def greet_mirror(n, carry):
        pr, pz, py = mirror_peer(n)

        @pl.when(jnp.logical_not(is_self(pr, pz, py)))
        def _():
            greet(at_plane(pr, pz, py))
        return carry

    @pl.when(z + 1 < height)
    def _():
        greet(at_plane(r, z + 1, y))

    @pl.when(z >= 1)
    def _():
        greet(at_plane(r, z - 1, y))

    greet(at_plane(r, z, 1 - y))
    lax.fori_loop(1, rows, greet_row, 0)
    lax.fori_loop(0, 2 * pairs * rows, greet_mirror, 0)
    lines_here = jnp.where(z + 1 < height, 1, 0) + jnp.where(z >= 1, 1, 0)
    selves = jnp.where(q == upper, 1, 0)
    pl.semaphore_wait(barrier, lines_here + rows + 2 * pairs * rows - selves)

    toward = 1 - 2 * q
    ways = (toward, -toward)

    def exists(plane):
        return jnp.logical_and(plane >= 0, plane < height)

    def sends(side, step, kind):
        way = ways[side]
        return jnp.logical_and(exists(z + way * (1 + kind)), exists(z - way * step))

    def receives(side, step, kind):
        way = ways[side]
        return jnp.logical_and(exists(z + way * (1 + step)), exists(z - way * kind))

    def came_from(side, step):
        return z + ways[side] * (1 + step)

    def line_copy(side, step, kind, m, incoming=False):
        way = ways[side]
        block = came_from(side, step) if incoming else z - way * step
        near, far = w_block(block, y, m), w_thru.at[block, m]
        place = near if kind == 0 else far
        if incoming:
            source = place
        elif step == 0:
            source = w_own(1 - q if kind == 0 else q, m)
        else:
            source = far if kind == 0 else near
        return remote(
            source, place, w_send.at[side, step, kind, m], w_recv.at[side, step, kind, m],
            at_plane(r, z + way, y))

    def send_line(side, step, kind, m):
        if step < height - 1:
            @pl.when(sends(side, step, kind))
            def _():
                line_copy(side, step, kind, m).start()

    def across(block, m, own=False):
        return remote(
            w_own(q, m) if own else w_block(block, y, m), w_block(block, y, m),
            wy_send.at[block, m], wy_recv.at[block, m], at_plane(r, z, 1 - y))

    def across_in(block, m):
        return remote(
            w_block(block, 1 - y, m), w_block(block, 1 - y, m),
            wy_send.at[block, m], wy_recv.at[block, m], at_plane(r, z, 1 - y))

    def relay(side, step, kind, phase, only=None):
        take = receives(side, step, kind)
        if only is not None:
            take = jnp.logical_and(take, only)

        @pl.when(take)
        def _():
            for n in range(many):
                m = chunk_of(phase, n, q if kind == 0 else 1 - q)
                line_copy(side, step, kind, m, True).wait_recv()
                if kind == 0:
                    across(came_from(side, step), m).start()
                send_line(1 - side, step + 1, 1 - kind, m)

    def send_own(side, kind, phase):
        for n in range(many):
            send_line(side, 0, kind, chunk_of(phase, n, 1 - q if kind == 0 else q))

    def across_own(phase):
        for n in range(many):
            across(z, chunk_of(phase, n, q), True).start()

    t_size = t_ref.shape[0] // pieces

    def t_rows(m):
        return pl.ds(m * t_size, t_size)

    def t_from(which, source_r, m):
        return t_all.at[which, source_r, t_rows(m), :]

    def t_copy(which, source_r, m, device, send, recv):
        return remote(t_from(which, source_r, m), t_from(which, source_r, m), send, recv, device)

    def t_row(k, d, m):
        which = q if k == 0 else 1 - q
        target = 2 * lax.rem(quad + d, quads) + core
        source = t_ref.at[t_rows(m), :] if k == 0 else t_from(which, r, m)
        return remote(source, t_from(which, r, m), t_send.at[k, d, m], t_recv.at[k, d, m], (target, c))

    def t_core(k, d, source_r, m):
        which = q if k == 0 else 1 - q
        source = t_ref.at[t_rows(m), :] if k == 0 and d == 0 else t_from(which, source_r, m)
        return remote(
            source, t_from(which, source_r, m), t_core_send.at[k, d, m], t_core_recv.at[k, d, m], (core_partner, c))

    def t_row_in(k, d, m):
        which = q if k == 0 else 1 - q
        source_r = 2 * lax.rem(quad + quads - d, quads) + core
        t_copy(which, source_r, m, (r, c), t_send.at[k, d, m], t_recv.at[k, d, m]).wait_recv()
        t_core(k, d, source_r, m).start()

    def t_rows_in(k, m):
        for d in range(1, quads):
            t_row_in(k, d, m)

    def t_plane(m):
        return remote(
            t_ref.at[t_rows(m), :], t_from(q, r, m), t_send.at[0, 0, m], t_recv.at[0, 0, m],
            at_plane(r, partner, y))

    def t_plane_in(m):
        t_copy(1 - q, r, m, at_plane(r, partner, y), t_send.at[0, 0, m], t_recv.at[0, 0, m]).wait_recv()
        for d in range(1, quads):
            t_row(1, d, m).start()
        t_core(1, 0, r, m).start()

    def wait_t_core(k):
        for d in range(quads):
            source_r = 2 * lax.rem(quad + quads - d, quads) + 1 - core
            for m in range(pieces):
                t_core(k, d, source_r, m).wait_recv()

    at_end = jnp.logical_or(z == 0, z == height - 1)
    inside = jnp.logical_not(at_end)

    for m in range(pieces):
        for d in range(1, quads):
            t_row(0, d, m).start()
    t_plane(0).start()
    across_own(0)
    send_own(1, 0, 0)
    send_own(1, 1, 0)
    send_own(0, 0, 0)
    send_own(0, 1, 0)

    @pl.when(at_end)
    def _():
        for m in range(1, pieces - 1):
            t_plane(m).start()
        send_own(0, 1, 1)
        t_plane(pieces - 1).start()
        send_own(0, 0, 1)
        across_own(1)

    for m in range(pieces):
        t_core(0, 0, r, m).start()

    tile = min(256, t_ref.shape[0])
    tiles = t_ref.shape[0] // tile

    def multiply(p, phase):
        def body(n, carry):
            at = pl.ds(pl.multiple_of(n % tiles * tile, tile), tile)
            m = chunk_of(phase, n // tiles, q)
            total = jnp.dot(t_all[p, 0, at, :], w_all[0, m], preferred_element_type=jnp.float32)
            for block in range(1, height):
                total += jnp.dot(t_all[p, block, at, :], w_all[block, m], preferred_element_type=jnp.float32)
            acc[p, m, at, :] = total
            return carry

        lax.fori_loop(0, many * tiles, body, 0)

    def w_ready(phase):
        for n in range(many):
            m = chunk_of(phase, n, q)
            w_local(m).wait()
            for block in range(height):
                across_in(block, m).wait_recv()

    def mirror_peer_at(j, m, py):
        s = m // 2 if parts == 2 else m
        return j, 2 * (q * pairs + s) + upper, py

    def mirror_part(m):
        return m % 2 if parts == 2 else 0

    def mirror_copy(g, j, m, py):
        part = mirror_part(m)
        return remote(
            enc.at[g, j, m, py], mirror.at[r, pair_here, y, g, part],
            m_send.at[g, j, m, py], m_recv.at[r, pair_here, y, g, part], at_plane(*mirror_peer_at(j, m, py)))

    def mirror_self(g, part):
        m = 2 * pair_here + part if parts == 2 else pair_here
        return pltpu.make_async_copy(
            enc.at[g, r, m, y], mirror.at[r, pair_here, y, g, part], local_sem.at[1 + 2 * g + part])

    def mirror_start(g, phase):
        def send_mirror(n, carry):
            j = lax.rem(r + n % occ + 1, occ)
            m = chunk_of(phase, n // occ, q)
            at = pl.ds(pl.multiple_of(j * vd, vd), vd)
            values = coded(acc[g, m, at, :], scale)
            for b in range(grouped):
                enc[g, j, m, b % 2, b // 2] = values[:, b * vd:(b + 1) * vd]
            for py in range(2):
                here = is_self(*mirror_peer_at(j, m, py))

                @pl.when(here)
                def _():
                    mirror_self(g, mirror_part(m)).start()

                @pl.when(jnp.logical_not(here))
                def _():
                    mirror_copy(g, j, m, py).start()
            return carry

        lax.fori_loop(0, many * occ, send_mirror, 0)

    def products(g, phase):
        multiply(g, phase)
        mirror_start(g, phase)

    def relay_rest(phase, least):
        for step in range(least, height - 1):
            relay(1, step, 0, phase)
            relay(0, step, 1, phase)
            relay(1, step, 1, phase)
            relay(0, step, 0, phase)

    t_local.wait()

    @pl.when(inside)
    def _():
        relay(1, 0, 0, 0)
        t_plane_in(0)
        t_rows_in(0, 0)
        relay(0, 0, 0, 0)
        relay(1, 0, 1, 0)
        t_plane(1).start()
        t_rows_in(0, 1)
        relay(0, 0, 1, 0)
        send_own(1, 0, 1)
        send_own(1, 1, 1)
        across_own(1)
        for m in range(2, pieces):
            t_rows_in(0, m)
        relay(1, 1, 1, 0)
        for m in range(2, pieces):
            t_plane(m).start()
        t_plane_in(1)
        relay(1, 1, 0, 0)
        send_own(0, 1, 1)
        send_own(0, 0, 1)
        if height > 4:
            relay(0, 1, 1, 0)
            relay(0, 1, 0, 0)
            relay_rest(0, 2)
        for m in range(2, pieces - 1):
            t_plane_in(m)
        t_rows_in(1, 0)
        relay(1, 0, 0, 1)
        relay(0, 0, 1, 1)
        relay(1, 0, 1, 1)
        w_ready(0)
        wait_t_core(0)
        products(q, 0)
        t_rows_in(1, 1)
        t_plane_in(pieces - 1)
        relay(1, 1, 0, 1)
        for m in range(2, pieces - 1):
            t_rows_in(1, m)
        relay(0, 0, 0, 1)
        t_rows_in(1, pieces - 1)
        relay(1, 1, 1, 1)
        if height > 4:
            relay(0, 1, 1, 1)
            relay(0, 1, 0, 1)
            relay_rest(1, 2)

        w_ready(1)
        products(q, 1)
        wait_t_core(1)
        products(1 - q, 1)
        products(1 - q, 0)

    @pl.when(at_end)
    def _():
        t_plane_in(0)
        relay(0, 0, 0, 0)
        t_rows_in(0, 0)
        t_rows_in(0, 1)
        relay(0, 1, 0, 0)
        for m in range(2, pieces - 1):
            t_rows_in(0, m)
        t_plane_in(1)
        t_rows_in(0, pieces - 1)
        for step in range(2, height - 1):
            relay(0, step, 0, 0)
        t_rows_in(1, 0)
        for m in range(2, pieces - 1):
            t_plane_in(m)
        t_rows_in(1, 1)
        w_ready(0)
        wait_t_core(0)
        products(q, 0)
        t_plane_in(pieces - 1)
        for m in range(2, pieces - 1):
            t_rows_in(1, m)
        relay(0, 0, 0, 1)
        t_rows_in(1, pieces - 1)
        for step in range(1, height - 1):
            relay(0, step, 0, 1)
        wait_t_core(1)
        products(1 - q, 0)
        w_ready(1)
        products(q, 1)
        products(1 - q, 1)

    lanes = max(128, vd)
    lines = width // lanes
    lines_all = 2 * half // lanes
    vir_mine = jnp.broadcast_to(evb_ref[pl.ds(c, 1), :], (lanes, vd)).T

    def write(j, h, place, value):
        for n in range(lines):
            line = (h * chunks + place) * lines + n
            gaps = (eo_ref[j] + eo_ref[r]) - vir_mine - eva_ref[pl.ds(line, 1), :]
            out_ref[pl.ds(j * lines_all + line, vd, stride=occ * lines_all), :] = (
                value[:, n * lanes:(n + 1) * lanes] / gaps)

    def update_copy(place, j):
        return remote(
            renc.at[place, j], rin.at[place, j], r_send.at[place, j], r_recv.at[place, j],
            at_plane(r, partner, y))

    def mirror_wait(j, s, py, g, part):
        sender = 2 * (q * pairs + s) + upper
        here = is_self(j, sender, py)

        @pl.when(here)
        def _():
            mirror_self(g, part).wait()

        @pl.when(jnp.logical_not(here))
        def _():
            remote(
                enc.at[g, 0, 0, py], mirror.at[j, s, py, g, part], m_send.at[g, 0, 0, py], m_recv.at[j, s, py, g, part],
                at_plane(j, sender, py)).wait_recv()

    def whole(p, place, j, theirs):
        at = pl.ds(pl.multiple_of(j * vd, vd), vd)
        return acc[p, place, at, :] + jnp.concatenate([decoded(x, scale).T for x in theirs], axis=1)

    def give(j, place, value):
        renc[place, j] = coded(value, scale)
        update_copy(place, j).start()

    def finish_parts(g, p):
        def body(n, carry):
            j = lax.rem(r + n % occ, occ)
            s = n // occ
            place = 2 * s + g
            for py in range(2):
                mirror_wait(j, s, py, g, p)
            value = whole(p, place, j, [mirror[j, s, py, g, p, 0] for py in range(2)])

            @pl.when(q == p)
            def _():
                write(j, q, place, value)

            @pl.when(q != p)
            def _():
                give(j, place, value)
            return carry

        lax.fori_loop(0, pairs * occ, body, 0)

    def finish_whole(n, carry):
        j = lax.rem(r + n % occ, occ)
        s = n // occ
        blocks = [(g, py) for g in range(2) for py in range(2)]
        for g, py in blocks:
            mirror_wait(j, s, py, g, 0)
        give(j, s, whole(1 - q, s, j, [mirror[j, s, py, g, 0, 1 - q] for g, py in blocks]))
        write(j, q, s, whole(q, s, j, [mirror[j, s, py, g, 0, q] for g, py in blocks]))
        return carry

    if parts == 2:
        def order(n, carry):
            g = jnp.where(jnp.where(inside, n // 2, n % 2) == 1, 1 - upper, upper)
            p = jnp.where(jnp.where(inside, n % 3 == 0, n < 2), 1 - upper, upper)
            finish_parts(g, p)
            return carry

        lax.fori_loop(0, 4, order, 0)
    else:
        lax.fori_loop(0, chunks * occ, finish_whole, 0)

    def last(n, carry):
        j = lax.rem(r + n, occ)
        place = lax.rem(n // occ + (upper if parts == 2 else 0), chunks)
        update_copy(place, j).wait_recv()
        write(j, 1 - q, place, decoded(rin[place, j], scale))
        return carry

    lax.fori_loop(0, chunks * occ, last, 0)

    def sent_update(n, carry):
        update_copy(n // occ, n % occ).wait_send()
        return carry

    lax.fori_loop(0, chunks * occ, sent_update, 0)

    def sent_mirror(n, carry):
        j, m = n // chunks, n % chunks
        for g in range(2):
            for py in range(2):
                @pl.when(jnp.logical_not(is_self(*mirror_peer_at(j, m, py))))
                def _():
                    mirror_copy(g, j, m, py).wait_send()
        return carry

    lax.fori_loop(0, chunks * occ, sent_mirror, 0)
    for m in range(chunks):
        for block in range(height):
            across(block, m).wait_send()
        for step in range(height - 1):
            for side in range(2):
                for kind in range(2):
                    @pl.when(sends(side, step, kind))
                    def _():
                        line_copy(side, step, kind, m).wait_send()
    for m in range(pieces):
        t_plane(m).wait_send()
        for k in range(2):
            for d in range(1, quads):
                t_row(k, d, m).wait_send()
            for d in range(quads):
                t_core(k, d, r, m).wait_send()


def on_device(rows, cols, w_inter, t_panel, amplitudes, e_occ, e_vir):
    kw, occ_dev, vir_all = w_inter.shape
    vd, occ, kt = t_panel.shape
    height = cols // 2
    bound = LARGEST_T * LARGEST_W * kw * cols
    scale = 2.0 ** math.floor(119.0 / POWER - math.log2(bound))
    w_matrix = w_inter.reshape(kw, vir_all)
    t_rows = jnp.transpose(t_panel, (1, 0, 2)).reshape(occ * vd, kt)
    half = vir_all // 2
    grouped = 2 if 2 * vd % 128 == 0 else 4
    width = grouped * vd
    chunks = half // width
    pairs = height // 4
    parts = 4 // grouped
    pieces = 4
    dma = pltpu.SemaphoreType.DMA
    vmem = pl.BlockSpec(memory_space=pltpu.VMEM)
    lanes = max(128, vd)
    smem = pl.BlockSpec(memory_space=pltpu.SMEM)
    update = pl.pallas_call(
        functools.partial(kernel, rows, height, scale),
        out_shape=jax.ShapeDtypeStruct((vd * occ * vir_all // lanes, lanes), jnp.float32),
        in_specs=[pl.BlockSpec(memory_space=pl.ANY), vmem, smem, vmem, vmem],
        out_specs=vmem,
        scratch_shapes=[
            pltpu.VMEM((height, chunks, 2 * kw, width), jnp.bfloat16),
            pltpu.VMEM((height, chunks, kw, width), jnp.bfloat16),
            pltpu.VMEM((2, rows, occ * vd, kt), jnp.bfloat16),
            pltpu.VMEM((2, chunks, occ * vd, width), jnp.float32),
            pltpu.VMEM((2, occ, chunks, 2, grouped // 2, vd, vd), jnp.bfloat16),
            pltpu.VMEM((rows, pairs, 2, 2, parts, grouped // 2, vd, vd), jnp.bfloat16),
            pltpu.VMEM((chunks, occ, vd, width), jnp.bfloat16),
            pltpu.VMEM((chunks, occ, vd, width), jnp.bfloat16),
            dma((5,)),
            dma((chunks,)),
            dma((2, height - 1, 2, chunks)),
            dma((2, height - 1, 2, chunks)),
            dma((height, chunks)),
            dma((height, chunks)),
            dma((2, rows // 2, pieces)),
            dma((2, rows // 2, pieces)),
            dma((2, rows // 2, pieces)),
            dma((2, rows // 2, pieces)),
            dma((2, occ, chunks, 2)),
            dma((rows, pairs, 2, 2, parts)),
            dma((chunks, occ)),
            dma((chunks, occ)),
        ],
        compiler_params=pltpu.CompilerParams(
            collective_id=0, has_side_effects=True, vmem_limit_bytes=28 * 1024 * 1024),
        name="amplitude_residual",
    )(w_matrix, t_rows, e_occ, e_vir.reshape(cols, vd), e_vir.reshape(vir_all // lanes, lanes))
    return (lax.optimization_barrier(amplitudes.reshape(update.shape)) + update).reshape(amplitudes.shape)


def solution(mesh):
    rows, cols = mesh.shape["row"], mesh.shape["col"]
    return jax.shard_map(
        functools.partial(on_device, rows, cols),
        mesh=mesh,
        in_specs=(
            P("col", "row", None),
            P("col", None, "row"),
            P("col", None, "row", None),
            P(),
            P(),
        ),
        out_specs=P("col", None, "row", None),
        check_vma=False,
    )
```

```python
import functools
import math

import jax
import jax.numpy as jnp
from jax import lax
from jax.experimental import pallas as pl
from jax.experimental.pallas import tpu as pltpu
from jax.sharding import PartitionSpec as P

MESH = pl.DeviceIdType.MESH
POWER = 7
LARGEST_T = 6.0
LARGEST_W = 0.109375


def coded(x, scale):
    x = x * scale
    x2 = x * x
    return (x2 * x2 * x2 * x).astype(jnp.bfloat16)


def decoded(y, scale):
    y = y.astype(jnp.float32)
    size = jnp.abs(y)
    root = jnp.exp2(jnp.log2(jnp.maximum(size, 1e-37)) * (1.0 / POWER)) * (1.0 / scale)
    root = jnp.where(size < 1e-37, 0.0, root)
    return jnp.where(y < 0, -root, root)


def kernel(
    rows, height, scale,
    w_ref, t_ref, eo_ref, evb_ref, eva_ref, out_ref,
    t_raw, w_all, w_thru, t_all, acc, enc, mirror, renc, rin,
    local_sem, w_sem, w_send, w_recv, wy_send, wy_recv,
    t_send, t_recv, t_core_send, t_core_recv, m_send, m_recv, r_send, r_recv,
):
    r = lax.axis_index("row")
    c = lax.axis_index("col")
    z, y = c // 2, c % 2
    q, pair = z % 2, z // 2
    partner = z + 1 - 2 * q
    upper = jnp.where(2 * z >= height, 1, 0)
    quads = rows // 2
    core, quad = r % 2, r // 2
    core_partner = r + 1 - 2 * core
    vd = evb_ref.shape[1]
    occ = eo_ref.shape[0]
    kw = w_ref.shape[0]
    half = height * vd
    pairs = height // 4
    pair_here = pair - upper * pairs
    chunks, width = acc.shape[1], acc.shape[3]
    grouped = width // vd
    parts = mirror.shape[4]
    pieces = t_send.shape[2]
    many = chunks // 2

    def remote(source, target, send, recv, device):
        return pltpu.make_async_remote_copy(source, target, send, recv, device_id=device, device_id_type=MESH)

    def at_plane(pr, pz, py):
        return (pr, 2 * pz + py)

    def chunk_of(phase, n, h):
        return 2 * n + jnp.where(h == 1, phase, 1 - phase) if parts == 2 else phase * many + n

    def w_own(h, m):
        return w_ref.at[:, pl.ds(pl.multiple_of(h * half + m * width, 128), width)]

    def w_block(block, part, m):
        return w_all.at[block, m, pl.ds(pl.multiple_of(part * kw, kw), kw), :]

    def w_local(m):
        return pltpu.make_async_copy(w_own(q, m), w_block(z, y, m), w_sem.at[m])

    t_local = pltpu.make_async_copy(t_ref, t_raw, local_sem.at[0])
    t_local.start()
    for m in range(chunks):
        w_local(m).start()

    barrier = pltpu.get_barrier_semaphore()

    def greet(device):
        pl.semaphore_signal(barrier, inc=1, device_id=device, device_id_type=MESH)

    def mirror_peer(n):
        pr, rest = n // (2 * pairs), n % (2 * pairs)
        return pr, 2 * (q * pairs + rest // 2) + upper, rest % 2

    def is_self(pr, pz, py):
        return jnp.logical_and(jnp.logical_and(pr == r, pz == z), py == y)

    def greet_row(d, carry):
        greet((lax.rem(r + d, rows), c))
        return carry

    def greet_mirror(n, carry):
        pr, pz, py = mirror_peer(n)

        @pl.when(jnp.logical_not(is_self(pr, pz, py)))
        def _():
            greet(at_plane(pr, pz, py))
        return carry

    @pl.when(z + 1 < height)
    def _():
        greet(at_plane(r, z + 1, y))

    @pl.when(z >= 1)
    def _():
        greet(at_plane(r, z - 1, y))

    greet(at_plane(r, z, 1 - y))
    lax.fori_loop(1, rows, greet_row, 0)
    lax.fori_loop(0, 2 * pairs * rows, greet_mirror, 0)
    lines_here = jnp.where(z + 1 < height, 1, 0) + jnp.where(z >= 1, 1, 0)
    selves = jnp.where(q == upper, 1, 0)
    t_local.wait()

    def by_occupied(n, carry):
        size = 16
        at = pl.ds(pl.multiple_of(n * size, size), size)
        values = jnp.transpose(t_raw[at], (1, 0, 2))
        for j in range(occ):
            t_all[q, r, pl.ds(pl.multiple_of(j * vd + n * size, size), size), :] = values[j]
        return carry

    lax.fori_loop(0, vd // 16, by_occupied, 0)
    pl.semaphore_wait(barrier, lines_here + rows + 2 * pairs * rows - selves)

    toward = 1 - 2 * q
    ways = (toward, -toward)

    def exists(plane):
        return jnp.logical_and(plane >= 0, plane < height)

    def sends(side, step, kind):
        way = ways[side]
        return jnp.logical_and(exists(z + way * (1 + kind)), exists(z - way * step))

    def receives(side, step, kind):
        way = ways[side]
        return jnp.logical_and(exists(z + way * (1 + step)), exists(z - way * kind))

    def came_from(side, step):
        return z + ways[side] * (1 + step)

    def line_copy(side, step, kind, m, incoming=False):
        way = ways[side]
        block = came_from(side, step) if incoming else z - way * step
        near, far = w_block(block, y, m), w_thru.at[block, m]
        place = near if kind == 0 else far
        if incoming:
            source = place
        elif step == 0:
            source = w_own(1 - q if kind == 0 else q, m)
        else:
            source = far if kind == 0 else near
        return remote(
            source, place, w_send.at[side, step, kind, m], w_recv.at[side, step, kind, m],
            at_plane(r, z + way, y))

    def send_line(side, step, kind, m):
        if step < height - 1:
            @pl.when(sends(side, step, kind))
            def _():
                line_copy(side, step, kind, m).start()

    def across(block, m, own=False):
        return remote(
            w_own(q, m) if own else w_block(block, y, m), w_block(block, y, m),
            wy_send.at[block, m], wy_recv.at[block, m], at_plane(r, z, 1 - y))

    def across_in(block, m):
        return remote(
            w_block(block, 1 - y, m), w_block(block, 1 - y, m),
            wy_send.at[block, m], wy_recv.at[block, m], at_plane(r, z, 1 - y))

    def relay(side, step, kind, phase, only=None):
        take = receives(side, step, kind)
        if only is not None:
            take = jnp.logical_and(take, only)

        @pl.when(take)
        def _():
            for n in range(many):
                m = chunk_of(phase, n, q if kind == 0 else 1 - q)
                line_copy(side, step, kind, m, True).wait_recv()
                if kind == 0:
                    across(came_from(side, step), m).start()
                send_line(1 - side, step + 1, 1 - kind, m)

    def send_own(side, kind, phase):
        for n in range(many):
            send_line(side, 0, kind, chunk_of(phase, n, 1 - q if kind == 0 else q))

    def across_own(phase):
        for n in range(many):
            across(z, chunk_of(phase, n, q), True).start()

    t_size = occ * vd // pieces

    def t_rows(m):
        return pl.ds(m * t_size, t_size)

    def t_from(which, source_r, m):
        return t_all.at[which, source_r, t_rows(m), :]

    def t_copy(which, source_r, m, device, send, recv):
        return remote(t_from(which, source_r, m), t_from(which, source_r, m), send, recv, device)

    def t_row(k, d, m):
        which = q if k == 0 else 1 - q
        target = 2 * lax.rem(quad + d, quads) + core
        return remote(t_from(which, r, m), t_from(which, r, m), t_send.at[k, d, m], t_recv.at[k, d, m], (target, c))

    def t_core(k, d, source_r, m):
        which = q if k == 0 else 1 - q
        return remote(
            t_from(which, source_r, m), t_from(which, source_r, m), t_core_send.at[k, d, m], t_core_recv.at[k, d, m], (core_partner, c))

    def t_row_in(k, d, m):
        which = q if k == 0 else 1 - q
        source_r = 2 * lax.rem(quad + quads - d, quads) + core
        t_copy(which, source_r, m, (r, c), t_send.at[k, d, m], t_recv.at[k, d, m]).wait_recv()
        t_core(k, d, source_r, m).start()

    def t_rows_in(k, m):
        for d in range(1, quads):
            t_row_in(k, d, m)

    def t_plane(m):
        return remote(
            t_from(q, r, m), t_from(q, r, m), t_send.at[0, 0, m], t_recv.at[0, 0, m],
            at_plane(r, partner, y))

    def t_plane_in(m):
        t_copy(1 - q, r, m, at_plane(r, partner, y), t_send.at[0, 0, m], t_recv.at[0, 0, m]).wait_recv()
        for d in range(1, quads):
            t_row(1, d, m).start()
        t_core(1, 0, r, m).start()

    def wait_t_core(k):
        for d in range(quads):
            source_r = 2 * lax.rem(quad + quads - d, quads) + 1 - core
            for m in range(pieces):
                t_core(k, d, source_r, m).wait_recv()

    at_end = jnp.logical_or(z == 0, z == height - 1)
    inside = jnp.logical_not(at_end)

    for m in range(pieces):
        for d in range(1, quads):
            t_row(0, d, m).start()
    t_plane(0).start()
    across_own(0)
    send_own(1, 0, 0)
    send_own(1, 1, 0)
    send_own(0, 0, 0)
    send_own(0, 1, 0)

    @pl.when(at_end)
    def _():
        for m in range(1, pieces - 1):
            t_plane(m).start()
        send_own(0, 1, 1)
        t_plane(pieces - 1).start()
        send_own(0, 0, 1)
        across_own(1)

    for m in range(pieces):
        t_core(0, 0, r, m).start()

    tile = min(256, occ * vd)
    tiles = occ * vd // tile

    def multiply(p, phase):
        def body(n, carry):
            at = pl.ds(pl.multiple_of(n % tiles * tile, tile), tile)
            m = chunk_of(phase, n // tiles, q)
            total = jnp.dot(t_all[p, 0, at, :], w_all[0, m], preferred_element_type=jnp.float32)
            for block in range(1, height):
                total += jnp.dot(t_all[p, block, at, :], w_all[block, m], preferred_element_type=jnp.float32)
            acc[p, m, at, :] = total
            return carry

        lax.fori_loop(0, many * tiles, body, 0)

    def w_ready(phase):
        for n in range(many):
            m = chunk_of(phase, n, q)
            w_local(m).wait()
            for block in range(height):
                across_in(block, m).wait_recv()

    def mirror_peer_at(j, m, py):
        s = m // 2 if parts == 2 else m
        return j, 2 * (q * pairs + s) + upper, py

    def mirror_part(m):
        return m % 2 if parts == 2 else 0

    def mirror_copy(g, j, m, py):
        part = mirror_part(m)
        return remote(
            enc.at[g, j, m, py], mirror.at[r, pair_here, y, g, part],
            m_send.at[g, j, m, py], m_recv.at[r, pair_here, y, g, part], at_plane(*mirror_peer_at(j, m, py)))

    def mirror_self(g, part):
        m = 2 * pair_here + part if parts == 2 else pair_here
        return pltpu.make_async_copy(
            enc.at[g, r, m, y], mirror.at[r, pair_here, y, g, part], local_sem.at[1 + 2 * g + part])

    def mirror_start(g, phase):
        def send_mirror(n, carry):
            j = lax.rem(r + n % occ + 1, occ)
            m = chunk_of(phase, n // occ, q)
            at = pl.ds(pl.multiple_of(j * vd, vd), vd)
            values = coded(acc[g, m, at, :], scale)
            for b in range(grouped):
                enc[g, j, m, b % 2, b // 2] = values[:, b * vd:(b + 1) * vd]
            for py in range(2):
                here = is_self(*mirror_peer_at(j, m, py))

                @pl.when(here)
                def _():
                    mirror_self(g, mirror_part(m)).start()

                @pl.when(jnp.logical_not(here))
                def _():
                    mirror_copy(g, j, m, py).start()
            return carry

        lax.fori_loop(0, many * occ, send_mirror, 0)

    def products(g, phase):
        multiply(g, phase)
        mirror_start(g, phase)

    def relay_rest(phase, least):
        for step in range(least, height - 1):
            relay(1, step, 0, phase)
            relay(0, step, 1, phase)
            relay(1, step, 1, phase)
            relay(0, step, 0, phase)

    @pl.when(inside)
    def _():
        relay(1, 0, 0, 0)
        t_plane_in(0)
        t_rows_in(0, 0)
        relay(0, 0, 0, 0)
        relay(1, 0, 1, 0)
        t_plane(1).start()
        t_rows_in(0, 1)
        relay(0, 0, 1, 0)
        send_own(1, 0, 1)
        send_own(1, 1, 1)
        across_own(1)
        for m in range(2, pieces):
            t_rows_in(0, m)
        relay(1, 1, 1, 0)
        for m in range(2, pieces):
            t_plane(m).start()
        t_plane_in(1)
        relay(1, 1, 0, 0)
        send_own(0, 1, 1)
        send_own(0, 0, 1)
        if height > 4:
            relay(0, 1, 1, 0)
            relay(0, 1, 0, 0)
            relay_rest(0, 2)
        for m in range(2, pieces - 1):
            t_plane_in(m)
        t_rows_in(1, 0)
        relay(1, 0, 0, 1)
        relay(0, 0, 1, 1)
        relay(1, 0, 1, 1)
        w_ready(0)
        wait_t_core(0)
        products(q, 0)
        t_rows_in(1, 1)
        t_plane_in(pieces - 1)
        relay(1, 1, 0, 1)
        for m in range(2, pieces - 1):
            t_rows_in(1, m)
        relay(0, 0, 0, 1)
        t_rows_in(1, pieces - 1)
        relay(1, 1, 1, 1)
        if height > 4:
            relay(0, 1, 1, 1)
            relay(0, 1, 0, 1)
            relay_rest(1, 2)

        w_ready(1)
        products(q, 1)
        wait_t_core(1)
        products(1 - q, 1)
        products(1 - q, 0)

    @pl.when(at_end)
    def _():
        t_plane_in(0)
        relay(0, 0, 0, 0)
        t_rows_in(0, 0)
        t_rows_in(0, 1)
        relay(0, 1, 0, 0)
        for m in range(2, pieces - 1):
            t_rows_in(0, m)
        t_plane_in(1)
        t_rows_in(0, pieces - 1)
        for step in range(2, height - 1):
            relay(0, step, 0, 0)
        t_rows_in(1, 0)
        for m in range(2, pieces - 1):
            t_plane_in(m)
        t_rows_in(1, 1)
        w_ready(0)
        wait_t_core(0)
        products(q, 0)
        t_plane_in(pieces - 1)
        for m in range(2, pieces - 1):
            t_rows_in(1, m)
        relay(0, 0, 0, 1)
        t_rows_in(1, pieces - 1)
        for step in range(1, height - 1):
            relay(0, step, 0, 1)
        wait_t_core(1)
        products(1 - q, 0)
        w_ready(1)
        products(q, 1)
        products(1 - q, 1)

    lanes = max(128, vd)
    lines = width // lanes
    lines_all = 2 * half // lanes
    vir_mine = jnp.broadcast_to(evb_ref[pl.ds(c, 1), :], (lanes, vd)).T

    def write(j, h, place, value):
        for n in range(lines):
            line = (h * chunks + place) * lines + n
            gaps = (eo_ref[j] + eo_ref[r]) - vir_mine - eva_ref[pl.ds(line, 1), :]
            out_ref[pl.ds(j * lines_all + line, vd, stride=occ * lines_all), :] = (
                value[:, n * lanes:(n + 1) * lanes] / gaps)

    def update_copy(place, j):
        return remote(
            renc.at[place, j], rin.at[place, j], r_send.at[place, j], r_recv.at[place, j],
            at_plane(r, partner, y))

    def mirror_wait(j, s, py, g, part):
        sender = 2 * (q * pairs + s) + upper
        here = is_self(j, sender, py)

        @pl.when(here)
        def _():
            mirror_self(g, part).wait()

        @pl.when(jnp.logical_not(here))
        def _():
            remote(
                enc.at[g, 0, 0, py], mirror.at[j, s, py, g, part], m_send.at[g, 0, 0, py], m_recv.at[j, s, py, g, part],
                at_plane(j, sender, py)).wait_recv()

    def whole(p, place, j, theirs):
        at = pl.ds(pl.multiple_of(j * vd, vd), vd)
        return acc[p, place, at, :] + jnp.concatenate([decoded(x, scale).T for x in theirs], axis=1)

    def give(j, place, value):
        renc[place, j] = coded(value, scale)
        update_copy(place, j).start()

    def finish_parts(g, p):
        def body(n, carry):
            j = lax.rem(r + n % occ, occ)
            s = n // occ
            place = 2 * s + g
            for py in range(2):
                mirror_wait(j, s, py, g, p)
            value = whole(p, place, j, [mirror[j, s, py, g, p, 0] for py in range(2)])

            @pl.when(q == p)
            def _():
                write(j, q, place, value)

            @pl.when(q != p)
            def _():
                give(j, place, value)
            return carry

        lax.fori_loop(0, pairs * occ, body, 0)

    def finish_whole(n, carry):
        j = lax.rem(r + n % occ, occ)
        s = n // occ
        blocks = [(g, py) for g in range(2) for py in range(2)]
        for g, py in blocks:
            mirror_wait(j, s, py, g, 0)
        give(j, s, whole(1 - q, s, j, [mirror[j, s, py, g, 0, 1 - q] for g, py in blocks]))
        write(j, q, s, whole(q, s, j, [mirror[j, s, py, g, 0, q] for g, py in blocks]))
        return carry

    if parts == 2:
        def order(n, carry):
            g = jnp.where(jnp.where(inside, n // 2, n % 2) == 1, 1 - upper, upper)
            p = jnp.where(jnp.where(inside, n % 3 == 0, n < 2), 1 - upper, upper)
            finish_parts(g, p)
            return carry

        lax.fori_loop(0, 4, order, 0)
    else:
        lax.fori_loop(0, chunks * occ, finish_whole, 0)

    def last(n, carry):
        j = lax.rem(r + n, occ)
        place = lax.rem(n // occ + (upper if parts == 2 else 0), chunks)
        update_copy(place, j).wait_recv()
        write(j, 1 - q, place, decoded(rin[place, j], scale))
        return carry

    lax.fori_loop(0, chunks * occ, last, 0)

    def sent_update(n, carry):
        update_copy(n // occ, n % occ).wait_send()
        return carry

    lax.fori_loop(0, chunks * occ, sent_update, 0)

    def sent_mirror(n, carry):
        j, m = n // chunks, n % chunks
        for g in range(2):
            for py in range(2):
                @pl.when(jnp.logical_not(is_self(*mirror_peer_at(j, m, py))))
                def _():
                    mirror_copy(g, j, m, py).wait_send()
        return carry

    lax.fori_loop(0, chunks * occ, sent_mirror, 0)
    for m in range(chunks):
        for block in range(height):
            across(block, m).wait_send()
        for step in range(height - 1):
            for side in range(2):
                for kind in range(2):
                    @pl.when(sends(side, step, kind))
                    def _():
                        line_copy(side, step, kind, m).wait_send()
    for m in range(pieces):
        t_plane(m).wait_send()
        for k in range(2):
            for d in range(1, quads):
                t_row(k, d, m).wait_send()
            for d in range(quads):
                t_core(k, d, r, m).wait_send()


def on_device(rows, cols, w_inter, t_panel, amplitudes, e_occ, e_vir):
    kw, occ_dev, vir_all = w_inter.shape
    vd, occ, kt = t_panel.shape
    height = cols // 2
    bound = LARGEST_T * LARGEST_W * kw * cols
    scale = 2.0 ** math.floor(119.0 / POWER - math.log2(bound))
    w_matrix = w_inter.reshape(kw, vir_all)
    half = vir_all // 2
    grouped = 2 if 2 * vd % 128 == 0 else 4
    width = grouped * vd
    chunks = half // width
    pairs = height // 4
    parts = 4 // grouped
    pieces = 4
    dma = pltpu.SemaphoreType.DMA
    vmem = pl.BlockSpec(memory_space=pltpu.VMEM)
    hbm = pl.BlockSpec(memory_space=pltpu.HBM)
    lanes = max(128, vd)
    smem = pl.BlockSpec(memory_space=pltpu.SMEM)
    update = pl.pallas_call(
        functools.partial(kernel, rows, height, scale),
        out_shape=pltpu.VMEM((vd * occ * vir_all // lanes, lanes), jnp.float32),
        in_specs=[hbm, hbm, smem, vmem, vmem],
        out_specs=vmem,
        scratch_shapes=[
            pltpu.VMEM((vd, occ, kt), jnp.bfloat16),
            pltpu.VMEM((height, chunks, 2 * kw, width), jnp.bfloat16),
            pltpu.VMEM((height, chunks, kw, width), jnp.bfloat16),
            pltpu.VMEM((2, rows, occ * vd, kt), jnp.bfloat16),
            pltpu.VMEM((2, chunks, occ * vd, width), jnp.float32),
            pltpu.VMEM((2, occ, chunks, 2, grouped // 2, vd, vd), jnp.bfloat16),
            pltpu.VMEM((rows, pairs, 2, 2, parts, grouped // 2, vd, vd), jnp.bfloat16),
            pltpu.VMEM((chunks, occ, vd, width), jnp.bfloat16),
            pltpu.VMEM((chunks, occ, vd, width), jnp.bfloat16),
            dma((5,)),
            dma((chunks,)),
            dma((2, height - 1, 2, chunks)),
            dma((2, height - 1, 2, chunks)),
            dma((height, chunks)),
            dma((height, chunks)),
            dma((2, rows // 2, pieces)),
            dma((2, rows // 2, pieces)),
            dma((2, rows // 2, pieces)),
            dma((2, rows // 2, pieces)),
            dma((2, occ, chunks, 2)),
            dma((rows, pairs, 2, 2, parts)),
            dma((chunks, occ)),
            dma((chunks, occ)),
        ],
        compiler_params=pltpu.CompilerParams(
            collective_id=0, has_side_effects=True, vmem_limit_bytes=int(56 * 1024 * 1024)),
        name="amplitude_residual",
    )(w_matrix, t_panel, e_occ, e_vir.reshape(cols, vd), e_vir.reshape(vir_all // lanes, lanes))
    return (lax.optimization_barrier(amplitudes.reshape(update.shape)) + update).reshape(amplitudes.shape)


def solution(mesh):
    rows, cols = mesh.shape["row"], mesh.shape["col"]
    return jax.shard_map(
        functools.partial(on_device, rows, cols),
        mesh=mesh,
        in_specs=(
            P("col", "row", None),
            P("col", None, "row"),
            P("col", None, "row", None),
            P(),
            P(),
        ),
        out_specs=P("col", None, "row", None),
        check_vma=False,
    )
```

```python
import functools
import math

import jax
import jax.numpy as jnp
from jax import lax
from jax.experimental import pallas as pl
from jax.experimental.pallas import tpu as pltpu
from jax.sharding import PartitionSpec as P

MESH = pl.DeviceIdType.MESH
POWER = 7
LARGEST_T = 6.0
LARGEST_W = 0.109375


def coded(x, scale):
    x = x * scale
    x2 = x * x
    return (x2 * x2 * x2 * x).astype(jnp.bfloat16)


def decoded(y, scale):
    y = y.astype(jnp.float32)
    size = jnp.abs(y)
    root = jnp.exp2(jnp.log2(jnp.maximum(size, 1e-37)) * (1.0 / POWER)) * (1.0 / scale)
    root = jnp.where(size < 1e-37, 0.0, root)
    return jnp.where(y < 0, -root, root)


def kernel(
    rows, height, scale,
    w_ref, t_ref, eo_ref, evb_ref, eva_ref, out_ref,
    t_raw, w_all, w_thru, t_all, acc, enc, mirror, renc, rin,
    local_sem, w_sem, w_send, w_recv, wy_send, wy_recv,
    t_send, t_recv, t_core_send, t_core_recv, m_send, m_recv, r_send, r_recv,
):
    r = lax.axis_index("row")
    c = lax.axis_index("col")
    z, y = c // 2, c % 2
    q, pair = z % 2, z // 2
    partner = z + 1 - 2 * q
    upper = jnp.where(2 * z >= height, 1, 0)
    quads = rows // 2
    core, quad = r % 2, r // 2
    core_partner = r + 1 - 2 * core
    vd = evb_ref.shape[1]
    occ = eo_ref.shape[0]
    kw = w_ref.shape[0]
    half = height * vd
    pairs = height // 4
    pair_here = pair - upper * pairs
    chunks, width = acc.shape[1], acc.shape[3]
    grouped = width // vd
    parts = mirror.shape[4]
    pieces = t_send.shape[2]
    many = chunks // 2

    def remote(source, target, send, recv, device):
        return pltpu.make_async_remote_copy(source, target, send, recv, device_id=device, device_id_type=MESH)

    def at_plane(pr, pz, py):
        return (pr, 2 * pz + py)

    def chunk_of(phase, n, h):
        return 2 * n + jnp.where(h == 1, phase, 1 - phase) if parts == 2 else phase * many + n

    def w_own(h, m):
        return w_ref.at[:, pl.ds(pl.multiple_of(h * half + m * width, 128), width)]

    def w_block(block, part, m):
        return w_all.at[block, m, pl.ds(pl.multiple_of(part * kw, kw), kw), :]

    cuts = wy_send.shape[2]

    def cut(ref, u):
        size = kw // cuts
        return ref.at[pl.ds(u * size, size), :]

    def w_local(m):
        return pltpu.make_async_copy(w_own(q, m), w_block(z, y, m), w_sem.at[m])

    t_local = pltpu.make_async_copy(t_ref, t_raw, local_sem.at[0])
    t_local.start()
    for m in range(chunks):
        w_local(m).start()

    barrier = pltpu.get_barrier_semaphore()

    def greet(device):
        pl.semaphore_signal(barrier, inc=1, device_id=device, device_id_type=MESH)

    def mirror_peer(n):
        pr, rest = n // (2 * pairs), n % (2 * pairs)
        return pr, 2 * (q * pairs + rest // 2) + upper, rest % 2

    def is_self(pr, pz, py):
        return jnp.logical_and(jnp.logical_and(pr == r, pz == z), py == y)

    def greet_row(d, carry):
        greet((lax.rem(r + d, rows), c))
        return carry

    def greet_mirror(n, carry):
        pr, pz, py = mirror_peer(n)

        @pl.when(jnp.logical_not(is_self(pr, pz, py)))
        def _():
            greet(at_plane(pr, pz, py))
        return carry

    @pl.when(z + 1 < height)
    def _():
        greet(at_plane(r, z + 1, y))

    @pl.when(z >= 1)
    def _():
        greet(at_plane(r, z - 1, y))

    greet(at_plane(r, z, 1 - y))
    lax.fori_loop(1, rows, greet_row, 0)
    lax.fori_loop(0, 2 * pairs * rows, greet_mirror, 0)
    lines_here = jnp.where(z + 1 < height, 1, 0) + jnp.where(z >= 1, 1, 0)
    selves = jnp.where(q == upper, 1, 0)
    t_local.wait()

    def by_occupied(n, carry):
        size = 16
        at = pl.ds(pl.multiple_of(n * size, size), size)
        values = jnp.transpose(t_raw[at], (1, 0, 2))
        for j in range(occ):
            t_all[q, r, pl.ds(pl.multiple_of(j * vd + n * size, size), size), :] = values[j]
        return carry

    lax.fori_loop(0, vd // 16, by_occupied, 0)
    pl.semaphore_wait(barrier, lines_here + rows + 2 * pairs * rows - selves)

    toward = 1 - 2 * q
    ways = (toward, -toward)

    def exists(plane):
        return jnp.logical_and(plane >= 0, plane < height)

    def sends(side, step, kind):
        way = ways[side]
        return jnp.logical_and(exists(z + way * (1 + kind)), exists(z - way * step))

    def receives(side, step, kind):
        way = ways[side]
        return jnp.logical_and(exists(z + way * (1 + step)), exists(z - way * kind))

    def came_from(side, step):
        return z + ways[side] * (1 + step)

    def line_copy(side, step, kind, m, u, incoming=False):
        way = ways[side]
        block = came_from(side, step) if incoming else z - way * step
        near, far = w_block(block, y, m), w_thru.at[block, m]
        place = near if kind == 0 else far
        if incoming:
            source = place
        elif step == 0:
            source = w_own(1 - q if kind == 0 else q, m)
        else:
            source = far if kind == 0 else near
        return remote(
            cut(source, u), cut(place, u), w_send.at[side, step, kind, m, u], w_recv.at[side, step, kind, m, u],
            at_plane(r, z + way, y))

    def send_line(side, step, kind, m, u):
        if step < height - 1:
            @pl.when(sends(side, step, kind))
            def _():
                line_copy(side, step, kind, m, u).start()

    def across(block, m, u, own=False):
        return remote(
            cut(w_own(q, m) if own else w_block(block, y, m), u), cut(w_block(block, y, m), u),
            wy_send.at[block, m, u], wy_recv.at[block, m, u], at_plane(r, z, 1 - y))

    def across_in(block, m, u):
        place = cut(w_block(block, 1 - y, m), u)
        return remote(place, place, wy_send.at[block, m, u], wy_recv.at[block, m, u], at_plane(r, z, 1 - y))

    def relay(side, step, kind, phase, only=None):
        take = receives(side, step, kind)
        if only is not None:
            take = jnp.logical_and(take, only)

        @pl.when(take)
        def _():
            for n in range(many):
                m = chunk_of(phase, n, q if kind == 0 else 1 - q)
                for u in range(cuts):
                    line_copy(side, step, kind, m, u, True).wait_recv()
                    send_line(1 - side, step + 1, 1 - kind, m, u)
                    if kind == 0:
                        across(came_from(side, step), m, u).start()

    def send_own(side, kind, phase):
        for n in range(many):
            for u in range(cuts):
                send_line(side, 0, kind, chunk_of(phase, n, 1 - q if kind == 0 else q), u)

    def across_own(phase):
        for n in range(many):
            for u in range(cuts):
                across(z, chunk_of(phase, n, q), u, True).start()

    t_size = occ * vd // pieces

    def t_rows(m):
        return pl.ds(m * t_size, t_size)

    def t_from(which, source_r, m):
        return t_all.at[which, source_r, t_rows(m), :]

    def t_copy(which, source_r, m, device, send, recv):
        return remote(t_from(which, source_r, m), t_from(which, source_r, m), send, recv, device)

    def t_row(k, d, m):
        which = q if k == 0 else 1 - q
        target = 2 * lax.rem(quad + d, quads) + core
        return remote(t_from(which, r, m), t_from(which, r, m), t_send.at[k, d, m], t_recv.at[k, d, m], (target, c))

    def t_core(k, d, source_r, m):
        which = q if k == 0 else 1 - q
        return remote(
            t_from(which, source_r, m), t_from(which, source_r, m), t_core_send.at[k, d, m], t_core_recv.at[k, d, m], (core_partner, c))

    def t_row_in(k, d, m):
        which = q if k == 0 else 1 - q
        source_r = 2 * lax.rem(quad + quads - d, quads) + core
        t_copy(which, source_r, m, (r, c), t_send.at[k, d, m], t_recv.at[k, d, m]).wait_recv()
        t_core(k, d, source_r, m).start()

    def t_rows_in(k, m):
        for d in range(1, quads):
            t_row_in(k, d, m)

    def t_plane(m):
        return remote(
            t_from(q, r, m), t_from(q, r, m), t_send.at[0, 0, m], t_recv.at[0, 0, m],
            at_plane(r, partner, y))

    def t_plane_in(m):
        t_copy(1 - q, r, m, at_plane(r, partner, y), t_send.at[0, 0, m], t_recv.at[0, 0, m]).wait_recv()
        for d in range(1, quads):
            t_row(1, d, m).start()
        t_core(1, 0, r, m).start()

    def wait_t_core(k):
        for d in range(quads):
            source_r = 2 * lax.rem(quad + quads - d, quads) + 1 - core
            for m in range(pieces):
                t_core(k, d, source_r, m).wait_recv()

    at_end = jnp.logical_or(z == 0, z == height - 1)
    inside = jnp.logical_not(at_end)

    for m in range(pieces):
        for d in range(1, quads):
            t_row(0, d, m).start()
    t_plane(0).start()
    across_own(0)
    send_own(1, 0, 0)
    send_own(1, 1, 0)
    send_own(0, 0, 0)
    send_own(0, 1, 0)

    @pl.when(at_end)
    def _():
        for m in range(1, pieces - 1):
            t_plane(m).start()
        send_own(0, 1, 1)
        t_plane(pieces - 1).start()
        send_own(0, 0, 1)
        across_own(1)

    for m in range(pieces):
        t_core(0, 0, r, m).start()

    tile = min(256, occ * vd)
    tiles = occ * vd // tile

    def w_ready(phase):
        for n in range(many):
            m = chunk_of(phase, n, q)
            w_local(m).wait()
            for block in range(height):
                for u in range(cuts):
                    across_in(block, m, u).wait_recv()

    def mirror_peer_at(j, m, py):
        s = m // 2 if parts == 2 else m
        return j, 2 * (q * pairs + s) + upper, py

    def mirror_part(m):
        return m % 2 if parts == 2 else 0

    def mirror_copy(g, j, m, py):
        part = mirror_part(m)
        return remote(
            enc.at[g, j, m, py], mirror.at[r, pair_here, y, g, part],
            m_send.at[g, j, m, py], m_recv.at[r, pair_here, y, g, part], at_plane(*mirror_peer_at(j, m, py)))

    def mirror_self(g, part):
        m = 2 * pair_here + part if parts == 2 else pair_here
        return pltpu.make_async_copy(
            enc.at[g, r, m, y], mirror.at[r, pair_here, y, g, part], local_sem.at[1 + 2 * g + part])

    def mirror_start(g, m, j):
        at = pl.ds(pl.multiple_of(j * vd, vd), vd)
        values = coded(acc[g, m, at, :], scale)
        for b in range(grouped):
            enc[g, j, m, b % 2, b // 2] = values[:, b * vd:(b + 1) * vd]
        for py in range(2):
            here = is_self(*mirror_peer_at(j, m, py))

            @pl.when(here)
            def _():
                mirror_self(g, mirror_part(m)).start()

            @pl.when(jnp.logical_not(here))
            def _():
                mirror_copy(g, j, m, py).start()

    def products(p, phase):
        first = 1 + r * tiles // rows

        def body(n, carry):
            place = lax.rem(n + first, tiles)
            at = pl.ds(pl.multiple_of(place * tile, tile), tile)
            m = chunk_of(phase, n // tiles, q)
            total = jnp.dot(t_all[p, 0, at, :], w_all[0, m], preferred_element_type=jnp.float32)
            for block in range(1, height):
                total += jnp.dot(t_all[p, block, at, :], w_all[block, m], preferred_element_type=jnp.float32)
            acc[p, m, at, :] = total
            for j in range(tile // vd):
                mirror_start(p, m, place * (tile // vd) + lax.rem(r + j + 1, tile // vd))
            return carry

        lax.fori_loop(0, many * tiles, body, 0)

    def relay_rest(phase, least):
        for step in range(least, height - 1):
            relay(1, step, 0, phase)
            relay(0, step, 1, phase)
            relay(1, step, 1, phase)
            relay(0, step, 0, phase)

    @pl.when(inside)
    def _():
        relay(1, 0, 0, 0)
        t_plane_in(0)
        t_rows_in(0, 0)
        relay(0, 0, 0, 0)
        relay(1, 0, 1, 0)
        t_plane(1).start()
        t_rows_in(0, 1)
        relay(0, 0, 1, 0)
        send_own(1, 0, 1)
        send_own(1, 1, 1)
        across_own(1)
        for m in range(2, pieces):
            t_rows_in(0, m)
        relay(1, 1, 1, 0)
        for m in range(2, pieces):
            t_plane(m).start()
        t_plane_in(1)
        relay(1, 1, 0, 0)
        send_own(0, 1, 1)
        send_own(0, 0, 1)
        if height > 4:
            relay(0, 1, 1, 0)
            relay(0, 1, 0, 0)
            relay_rest(0, 2)
        for m in range(2, pieces - 1):
            t_plane_in(m)
        t_rows_in(1, 0)
        relay(1, 0, 0, 1)
        relay(0, 0, 1, 1)
        relay(1, 0, 1, 1)
        t_rows_in(1, 1)
        t_plane_in(pieces - 1)
        relay(1, 1, 0, 1)
        for m in range(2, pieces - 1):
            t_rows_in(1, m)
        relay(0, 0, 0, 1)
        t_rows_in(1, pieces - 1)
        w_ready(0)
        wait_t_core(0)
        products(q, 0)
        relay(1, 1, 1, 1)
        if height > 4:
            relay(0, 1, 1, 1)
            relay(0, 1, 0, 1)
            relay_rest(1, 2)

        w_ready(1)
        products(q, 1)
        wait_t_core(1)
        products(1 - q, 1)
        products(1 - q, 0)

    @pl.when(at_end)
    def _():
        t_plane_in(0)
        relay(0, 0, 0, 0)
        t_rows_in(0, 0)
        t_rows_in(0, 1)
        relay(0, 1, 0, 0)
        for m in range(2, pieces - 1):
            t_rows_in(0, m)
        t_plane_in(1)
        t_rows_in(0, pieces - 1)
        for step in range(2, height - 1):
            relay(0, step, 0, 0)
        t_rows_in(1, 0)
        for m in range(2, pieces - 1):
            t_plane_in(m)
        t_rows_in(1, 1)
        w_ready(0)
        wait_t_core(0)
        products(q, 0)
        t_plane_in(pieces - 1)
        for m in range(2, pieces - 1):
            t_rows_in(1, m)
        relay(0, 0, 0, 1)
        t_rows_in(1, pieces - 1)
        for step in range(1, height - 1):
            relay(0, step, 0, 1)
        wait_t_core(1)
        products(1 - q, 0)
        w_ready(1)
        products(q, 1)
        products(1 - q, 1)

    for m in range(chunks):
        for block in range(height):
            for u in range(cuts):
                across(block, m, u).wait_send()
        for step in range(height - 1):
            for side in range(2):
                for kind in range(2):
                    @pl.when(sends(side, step, kind))
                    def _():
                        for u in range(cuts):
                            line_copy(side, step, kind, m, u).wait_send()
    for m in range(pieces):
        t_plane(m).wait_send()
        for k in range(2):
            for d in range(1, quads):
                t_row(k, d, m).wait_send()
            for d in range(quads):
                t_core(k, d, r, m).wait_send()

    lanes = max(128, vd)
    lines = width // lanes
    lines_all = 2 * half // lanes
    vir_mine = jnp.broadcast_to(evb_ref[pl.ds(c, 1), :], (lanes, vd)).T

    def write(j, h, place, value):
        for n in range(lines):
            line = (h * chunks + place) * lines + n
            gaps = (eo_ref[j] + eo_ref[r]) - vir_mine - eva_ref[pl.ds(line, 1), :]
            out_ref[pl.ds(j * lines_all + line, vd, stride=occ * lines_all), :] = (
                value[:, n * lanes:(n + 1) * lanes] / gaps)

    def update_copy(place, j):
        return remote(
            renc.at[place, j], rin.at[place, j], r_send.at[place, j], r_recv.at[place, j],
            at_plane(r, partner, y))

    def mirror_wait(j, s, py, g, part):
        sender = 2 * (q * pairs + s) + upper
        here = is_self(j, sender, py)

        @pl.when(here)
        def _():
            mirror_self(g, part).wait()

        @pl.when(jnp.logical_not(here))
        def _():
            remote(
                enc.at[g, 0, 0, py], mirror.at[j, s, py, g, part], m_send.at[g, 0, 0, py], m_recv.at[j, s, py, g, part],
                at_plane(j, sender, py)).wait_recv()

    def whole(p, place, j, theirs):
        at = pl.ds(pl.multiple_of(j * vd, vd), vd)
        return acc[p, place, at, :] + jnp.concatenate([decoded(x, scale).T for x in theirs], axis=1)

    def give(j, place, value):
        renc[place, j] = coded(value, scale)
        update_copy(place, j).start()

    def finish_parts(g, p):
        def body(n, carry):
            j = lax.rem(r + n % occ, occ)
            s = n // occ
            place = 2 * s + g
            for py in range(2):
                mirror_wait(j, s, py, g, p)
            value = whole(p, place, j, [mirror[j, s, py, g, p, 0] for py in range(2)])

            @pl.when(q == p)
            def _():
                write(j, q, place, value)

            @pl.when(q != p)
            def _():
                give(j, place, value)
            return carry

        lax.fori_loop(0, pairs * occ, body, 0)

    def finish_whole(n, carry):
        j = lax.rem(r + n % occ, occ)
        s = n // occ
        blocks = [(g, py) for g in range(2) for py in range(2)]
        for g, py in blocks:
            mirror_wait(j, s, py, g, 0)
        give(j, s, whole(1 - q, s, j, [mirror[j, s, py, g, 0, 1 - q] for g, py in blocks]))
        write(j, q, s, whole(q, s, j, [mirror[j, s, py, g, 0, q] for g, py in blocks]))
        return carry

    if parts == 2:
        def order(n, carry):
            g = jnp.where(jnp.where(inside, n // 2, n % 2) == 1, 1 - upper, upper)
            p = jnp.where(jnp.where(inside, n % 3 == 0, n < 2), 1 - upper, upper)
            finish_parts(g, p)
            return carry

        lax.fori_loop(0, 4, order, 0)
    else:
        lax.fori_loop(0, chunks * occ, finish_whole, 0)

    def sent_mirror(n, carry):
        j, m = n // chunks, n % chunks
        for g in range(2):
            for py in range(2):
                @pl.when(jnp.logical_not(is_self(*mirror_peer_at(j, m, py))))
                def _():
                    mirror_copy(g, j, m, py).wait_send()
        return carry

    lax.fori_loop(0, chunks * occ, sent_mirror, 0)

    def last(n, carry):
        j = lax.rem(r + n, occ)
        place = lax.rem(n // occ + (upper if parts == 2 else 0), chunks)
        update_copy(place, j).wait_recv()
        write(j, 1 - q, place, decoded(rin[place, j], scale))
        return carry

    lax.fori_loop(0, chunks * occ, last, 0)

    def sent_update(n, carry):
        update_copy(n // occ, n % occ).wait_send()
        return carry

    lax.fori_loop(0, chunks * occ, sent_update, 0)


def on_device(rows, cols, w_inter, t_panel, amplitudes, e_occ, e_vir):
    kw, occ_dev, vir_all = w_inter.shape
    vd, occ, kt = t_panel.shape
    height = cols // 2
    bound = LARGEST_T * LARGEST_W * kw * cols
    scale = 2.0 ** math.floor(119.0 / POWER - math.log2(bound))
    w_matrix = w_inter.reshape(kw, vir_all)
    half = vir_all // 2
    grouped = 2 if 2 * vd % 128 == 0 else 4
    width = grouped * vd
    chunks = half // width
    pairs = height // 4
    parts = 4 // grouped
    pieces = 4
    cuts = 2 if kw % 32 == 0 else 1
    dma = pltpu.SemaphoreType.DMA
    vmem = pl.BlockSpec(memory_space=pltpu.VMEM)
    hbm = pl.BlockSpec(memory_space=pltpu.HBM)
    lanes = max(128, vd)
    smem = pl.BlockSpec(memory_space=pltpu.SMEM)
    update = pl.pallas_call(
        functools.partial(kernel, rows, height, scale),
        out_shape=pltpu.VMEM((vd * occ * vir_all // lanes, lanes), jnp.float32),
        in_specs=[hbm, hbm, smem, vmem, vmem],
        out_specs=vmem,
        scratch_shapes=[
            pltpu.VMEM((vd, occ, kt), jnp.bfloat16),
            pltpu.VMEM((height, chunks, 2 * kw, width), jnp.bfloat16),
            pltpu.VMEM((height, chunks, kw, width), jnp.bfloat16),
            pltpu.VMEM((2, rows, occ * vd, kt), jnp.bfloat16),
            pltpu.VMEM((2, chunks, occ * vd, width), jnp.float32),
            pltpu.VMEM((2, occ, chunks, 2, grouped // 2, vd, vd), jnp.bfloat16),
            pltpu.VMEM((rows, pairs, 2, 2, parts, grouped // 2, vd, vd), jnp.bfloat16),
            pltpu.VMEM((chunks, occ, vd, width), jnp.bfloat16),
            pltpu.VMEM((chunks, occ, vd, width), jnp.bfloat16),
            dma((5,)),
            dma((chunks,)),
            dma((2, height - 1, 2, chunks, cuts)),
            dma((2, height - 1, 2, chunks, cuts)),
            dma((height, chunks, cuts)),
            dma((height, chunks, cuts)),
            dma((2, rows // 2, pieces)),
            dma((2, rows // 2, pieces)),
            dma((2, rows // 2, pieces)),
            dma((2, rows // 2, pieces)),
            dma((2, occ, chunks, 2)),
            dma((rows, pairs, 2, 2, parts)),
            dma((chunks, occ)),
            dma((chunks, occ)),
        ],
        compiler_params=pltpu.CompilerParams(
            collective_id=0, has_side_effects=True, vmem_limit_bytes=int(56 * 1024 * 1024)),
        name="amplitude_residual",
    )(w_matrix, t_panel, e_occ, e_vir.reshape(cols, vd), e_vir.reshape(vir_all // lanes, lanes))
    return (lax.optimization_barrier(amplitudes.reshape(update.shape)) + update).reshape(amplitudes.shape)


def solution(mesh):
    rows, cols = mesh.shape["row"], mesh.shape["col"]
    return jax.shard_map(
        functools.partial(on_device, rows, cols),
        mesh=mesh,
        in_specs=(
            P("col", "row", None),
            P("col", None, "row"),
            P("col", None, "row", None),
            P(),
            P(),
        ),
        out_specs=P("col", None, "row", None),
        check_vma=False,
    )
```

```python
import functools
import math

import jax
import jax.numpy as jnp
from jax import lax
from jax.experimental import pallas as pl
from jax.experimental.pallas import tpu as pltpu
from jax.sharding import PartitionSpec as P

MESH = pl.DeviceIdType.MESH
POWER = 7
LARGEST_T = 6.0
LARGEST_W = 0.109375


def coded(x, scale):
    x = x * scale
    x2 = x * x
    return (x2 * x2 * x2 * x).astype(jnp.bfloat16)


def decoded(y, scale):
    y = y.astype(jnp.float32)
    size = jnp.abs(y)
    root = jnp.exp2(jnp.log2(jnp.maximum(size, 1e-37)) * (1.0 / POWER)) * (1.0 / scale)
    root = jnp.where(size < 1e-37, 0.0, root)
    return jnp.where(y < 0, -root, root)


def kernel(
    rows, height, scale,
    w_ref, t_ref, eo_ref, evb_ref, eva_ref, out_ref,
    t_raw, w_all, w_thru, t_all, acc, enc, mirror, renc, rin,
    local_sem, w_sem, w_send, w_recv, wy_send, wy_recv,
    t_send, t_recv, t_core_send, t_core_recv, m_send, m_recv, r_send, r_recv,
):
    r = lax.axis_index("row")
    c = lax.axis_index("col")
    z, y = c // 2, c % 2
    q, pair = z % 2, z // 2
    partner = z + 1 - 2 * q
    upper = jnp.where(2 * z >= height, 1, 0)
    quads = rows // 2
    core, quad = r % 2, r // 2
    core_partner = r + 1 - 2 * core
    vd = evb_ref.shape[1]
    occ = eo_ref.shape[0]
    kw = w_ref.shape[0]
    half = height * vd
    pairs = height // 4
    pair_here = pair - upper * pairs
    chunks, width = acc.shape[1], acc.shape[3]
    grouped = width // vd
    parts = mirror.shape[4]
    pieces = t_send.shape[2]
    many = chunks // 2

    def remote(source, target, send, recv, device):
        return pltpu.make_async_remote_copy(source, target, send, recv, device_id=device, device_id_type=MESH)

    def at_plane(pr, pz, py):
        return (pr, 2 * pz + py)

    def chunk_of(phase, n, h):
        return 2 * n + jnp.where(h == 1, phase, 1 - phase) if parts == 2 else phase * many + n

    def w_own(h, m):
        return w_ref.at[:, pl.ds(pl.multiple_of(h * half + m * width, 128), width)]

    def w_block(block, part, m):
        return w_all.at[block, m, pl.ds(pl.multiple_of(part * kw, kw), kw), :]

    cuts = wy_send.shape[2]

    def cut(ref, u):
        size = kw // cuts
        return ref.at[pl.ds(u * size, size), :]

    def w_local(m):
        return pltpu.make_async_copy(w_own(q, m), w_block(z, y, m), w_sem.at[m])

    t_local = pltpu.make_async_copy(t_ref, t_raw, local_sem.at[0])
    t_local.start()
    for m in range(chunks):
        w_local(m).start()

    barrier = pltpu.get_barrier_semaphore()

    def greet(device):
        pl.semaphore_signal(barrier, inc=1, device_id=device, device_id_type=MESH)

    def mirror_peer(n):
        pr, rest = n // (2 * pairs), n % (2 * pairs)
        return pr, 2 * (q * pairs + rest // 2) + upper, rest % 2

    def is_self(pr, pz, py):
        return jnp.logical_and(jnp.logical_and(pr == r, pz == z), py == y)

    def greet_row(d, carry):
        greet((lax.rem(r + d, rows), c))
        return carry

    def greet_mirror(n, carry):
        pr, pz, py = mirror_peer(n)

        @pl.when(jnp.logical_not(is_self(pr, pz, py)))
        def _():
            greet(at_plane(pr, pz, py))
        return carry

    @pl.when(z + 1 < height)
    def _():
        greet(at_plane(r, z + 1, y))

    @pl.when(z >= 1)
    def _():
        greet(at_plane(r, z - 1, y))

    greet(at_plane(r, z, 1 - y))
    lax.fori_loop(1, rows, greet_row, 0)
    lax.fori_loop(0, 2 * pairs * rows, greet_mirror, 0)
    lines_here = jnp.where(z + 1 < height, 1, 0) + jnp.where(z >= 1, 1, 0)
    selves = jnp.where(q == upper, 1, 0)
    t_local.wait()

    def by_occupied(n, carry):
        size = 16
        at = pl.ds(pl.multiple_of(n * size, size), size)
        values = jnp.transpose(t_raw[at], (1, 0, 2))
        for j in range(occ):
            t_all[q, r, pl.ds(pl.multiple_of(j * vd + n * size, size), size), :] = values[j]
        return carry

    lax.fori_loop(0, vd // 16, by_occupied, 0)
    pl.semaphore_wait(barrier, lines_here + rows + 2 * pairs * rows - selves)

    toward = 1 - 2 * q
    ways = (toward, -toward)

    def exists(plane):
        return jnp.logical_and(plane >= 0, plane < height)

    def sends(side, step, kind):
        way = ways[side]
        return jnp.logical_and(exists(z + way * (1 + kind)), exists(z - way * step))

    def receives(side, step, kind):
        way = ways[side]
        return jnp.logical_and(exists(z + way * (1 + step)), exists(z - way * kind))

    def came_from(side, step):
        return z + ways[side] * (1 + step)

    def line_copy(side, step, kind, m, u, incoming=False):
        way = ways[side]
        block = came_from(side, step) if incoming else z - way * step
        near, far = w_block(block, y, m), w_thru.at[block, m]
        place = near if kind == 0 else far
        if incoming:
            source = place
        elif step == 0:
            source = w_own(1 - q if kind == 0 else q, m)
        else:
            source = far if kind == 0 else near
        return remote(
            cut(source, u), cut(place, u), w_send.at[side, step, kind, m, u], w_recv.at[side, step, kind, m, u],
            at_plane(r, z + way, y))

    def send_line(side, step, kind, m, u):
        if step < height - 1:
            @pl.when(sends(side, step, kind))
            def _():
                line_copy(side, step, kind, m, u).start()

    def across(block, m, u, own=False):
        return remote(
            cut(w_own(q, m) if own else w_block(block, y, m), u), cut(w_block(block, y, m), u),
            wy_send.at[block, m, u], wy_recv.at[block, m, u], at_plane(r, z, 1 - y))

    def across_in(block, m, u):
        place = cut(w_block(block, 1 - y, m), u)
        return remote(place, place, wy_send.at[block, m, u], wy_recv.at[block, m, u], at_plane(r, z, 1 - y))

    def relay(side, step, kind, phase, only=None):
        take = receives(side, step, kind)
        if only is not None:
            take = jnp.logical_and(take, only)

        @pl.when(take)
        def _():
            for n in range(many):
                m = chunk_of(phase, n, q if kind == 0 else 1 - q)
                for u in range(cuts):
                    line_copy(side, step, kind, m, u, True).wait_recv()
                    send_line(1 - side, step + 1, 1 - kind, m, u)
                    if kind == 0:
                        across(came_from(side, step), m, u).start()

    def send_own(side, kind, phase):
        for n in range(many):
            for u in range(cuts):
                send_line(side, 0, kind, chunk_of(phase, n, 1 - q if kind == 0 else q), u)

    def across_own(phase):
        for n in range(many):
            for u in range(cuts):
                across(z, chunk_of(phase, n, q), u, True).start()

    t_size = occ * vd // pieces

    def t_rows(m):
        return pl.ds(m * t_size, t_size)

    def t_from(which, source_r, m):
        return t_all.at[which, source_r, t_rows(m), :]

    def t_copy(which, source_r, m, device, send, recv):
        return remote(t_from(which, source_r, m), t_from(which, source_r, m), send, recv, device)

    def t_row(k, d, m):
        which = q if k == 0 else 1 - q
        target = 2 * lax.rem(quad + d, quads) + core
        return remote(t_from(which, r, m), t_from(which, r, m), t_send.at[k, d, m], t_recv.at[k, d, m], (target, c))

    def t_core(k, d, source_r, m):
        which = q if k == 0 else 1 - q
        return remote(
            t_from(which, source_r, m), t_from(which, source_r, m), t_core_send.at[k, d, m], t_core_recv.at[k, d, m], (core_partner, c))

    def t_row_in(k, d, m):
        which = q if k == 0 else 1 - q
        source_r = 2 * lax.rem(quad + quads - d, quads) + core
        t_copy(which, source_r, m, (r, c), t_send.at[k, d, m], t_recv.at[k, d, m]).wait_recv()
        t_core(k, d, source_r, m).start()

    def t_rows_in(k, m):
        for d in range(1, quads):
            t_row_in(k, d, m)

    def t_plane(m):
        return remote(
            t_from(q, r, m), t_from(q, r, m), t_send.at[0, 0, m], t_recv.at[0, 0, m],
            at_plane(r, partner, y))

    def t_plane_in(m):
        t_copy(1 - q, r, m, at_plane(r, partner, y), t_send.at[0, 0, m], t_recv.at[0, 0, m]).wait_recv()
        for d in range(1, quads):
            t_row(1, d, m).start()
        t_core(1, 0, r, m).start()

    def wait_t_core(k):
        for d in range(quads):
            source_r = 2 * lax.rem(quad + quads - d, quads) + 1 - core
            for m in range(pieces):
                t_core(k, d, source_r, m).wait_recv()

    at_end = jnp.logical_or(z == 0, z == height - 1)
    inside = jnp.logical_not(at_end)

    t_plane(0).start()
    send_own(1, 0, 0)
    across_own(0)
    for d in range(1, quads):
        t_row(0, d, 0).start()
    send_own(0, 0, 0)
    send_own(1, 1, 0)
    send_own(0, 1, 0)
    for m in range(1, pieces):
        for d in range(1, quads):
            t_row(0, d, m).start()

    @pl.when(at_end)
    def _():
        for m in range(1, pieces - 1):
            t_plane(m).start()
        send_own(0, 1, 1)
        t_plane(pieces - 1).start()
        send_own(0, 0, 1)
        across_own(1)

    for m in range(pieces):
        t_core(0, 0, r, m).start()

    tile = min(256, occ * vd)
    tiles = occ * vd // tile

    def w_ready(phase):
        for n in range(many):
            m = chunk_of(phase, n, q)
            w_local(m).wait()
            for block in range(height):
                for u in range(cuts):
                    across_in(block, m, u).wait_recv()

    def mirror_peer_at(j, m, py):
        s = m // 2 if parts == 2 else m
        return j, 2 * (q * pairs + s) + upper, py

    def mirror_part(m):
        return m % 2 if parts == 2 else 0

    def mirror_copy(g, j, m, py):
        part = mirror_part(m)
        return remote(
            enc.at[g, j, m, py], mirror.at[r, pair_here, y, g, part],
            m_send.at[g, j, m, py], m_recv.at[r, pair_here, y, g, part], at_plane(*mirror_peer_at(j, m, py)))

    def mirror_self(g, part):
        m = 2 * pair_here + part if parts == 2 else pair_here
        return pltpu.make_async_copy(
            enc.at[g, r, m, y], mirror.at[r, pair_here, y, g, part], local_sem.at[1 + 2 * g + part])

    def mirror_start(g, m, j):
        at = pl.ds(pl.multiple_of(j * vd, vd), vd)
        values = coded(acc[g, m, at, :], scale)
        for b in range(grouped):
            enc[g, j, m, b % 2, b // 2] = values[:, b * vd:(b + 1) * vd]
        for py in range(2):
            here = is_self(*mirror_peer_at(j, m, py))

            @pl.when(here)
            def _():
                mirror_self(g, mirror_part(m)).start()

            @pl.when(jnp.logical_not(here))
            def _():
                mirror_copy(g, j, m, py).start()

    def products(p, phase):
        first = 1 + r * tiles // rows

        def body(n, carry):
            place = lax.rem(n + first, tiles)
            at = pl.ds(pl.multiple_of(place * tile, tile), tile)
            m = chunk_of(phase, n // tiles, q)
            total = jnp.dot(t_all[p, 0, at, :], w_all[0, m], preferred_element_type=jnp.float32)
            for block in range(1, height):
                total += jnp.dot(t_all[p, block, at, :], w_all[block, m], preferred_element_type=jnp.float32)
            acc[p, m, at, :] = total
            for j in range(tile // vd):
                mirror_start(p, m, place * (tile // vd) + lax.rem(r + j + 1, tile // vd))
            return carry

        lax.fori_loop(0, many * tiles, body, 0)

    def relay_rest(phase, least):
        for step in range(least, height - 1):
            relay(1, step, 0, phase)
            relay(0, step, 1, phase)
            relay(1, step, 1, phase)
            relay(0, step, 0, phase)

    lanes = max(128, vd)
    lines = width // lanes
    lines_all = 2 * half // lanes
    vir_mine = jnp.broadcast_to(evb_ref[pl.ds(c, 1), :], (lanes, vd)).T

    def write(j, h, place, value):
        for n in range(lines):
            line = (h * chunks + place) * lines + n
            gaps = (eo_ref[j] + eo_ref[r]) - vir_mine - eva_ref[pl.ds(line, 1), :]
            out_ref[pl.ds(j * lines_all + line, vd, stride=occ * lines_all), :] = (
                value[:, n * lanes:(n + 1) * lanes] / gaps)

    def update_copy(place, j):
        return remote(
            renc.at[place, j], rin.at[place, j], r_send.at[place, j], r_recv.at[place, j],
            at_plane(r, partner, y))

    def mirror_wait(j, s, py, g, part):
        sender = 2 * (q * pairs + s) + upper
        here = is_self(j, sender, py)

        @pl.when(here)
        def _():
            mirror_self(g, part).wait()

        @pl.when(jnp.logical_not(here))
        def _():
            remote(
                enc.at[g, 0, 0, py], mirror.at[j, s, py, g, part], m_send.at[g, 0, 0, py], m_recv.at[j, s, py, g, part],
                at_plane(j, sender, py)).wait_recv()

    def whole(p, place, j, theirs):
        at = pl.ds(pl.multiple_of(j * vd, vd), vd)
        return acc[p, place, at, :] + jnp.concatenate([decoded(x.T, scale) for x in theirs], axis=1)

    def give(j, place, value):
        renc[place, j] = coded(value, scale)
        update_copy(place, j).start()

    def finish_parts(g, p):
        def body(n, carry):
            j = lax.rem(r + n % occ, occ)
            s = n // occ
            place = 2 * s + g
            for py in range(2):
                mirror_wait(j, s, py, g, p)
            value = whole(p, place, j, [mirror[j, s, py, g, p, 0] for py in range(2)])

            @pl.when(q == p)
            def _():
                write(j, q, place, value)

            @pl.when(q != p)
            def _():
                give(j, place, value)
            return carry

        lax.fori_loop(0, pairs * occ, body, 0)

    def finish_whole(n, carry):
        j = lax.rem(r + n % occ, occ)
        s = n // occ
        blocks = [(g, py) for g in range(2) for py in range(2)]
        for g, py in blocks:
            mirror_wait(j, s, py, g, 0)
        give(j, s, whole(1 - q, s, j, [mirror[j, s, py, g, 0, 1 - q] for g, py in blocks]))
        write(j, q, s, whole(q, s, j, [mirror[j, s, py, g, 0, q] for g, py in blocks]))
        return carry

    def finish_next(n, carry):
        g = jnp.where(jnp.where(inside, n >= 2, n % 3 == 0), 1 - upper, upper)
        p = jnp.where(jnp.where(inside, n % 3 == 0, n < 2), 1 - upper, upper)
        finish_parts(g, p)
        return carry

    def finish_first():
        if parts == 2:
            finish_next(0, 0)

    @pl.when(inside)
    def _():
        relay(1, 0, 0, 0)
        t_plane_in(0)
        t_rows_in(0, 0)
        relay(0, 0, 0, 0)
        relay(1, 0, 1, 0)
        t_plane(1).start()
        t_rows_in(0, 1)
        relay(0, 0, 1, 0)
        send_own(1, 0, 1)
        send_own(1, 1, 1)
        across_own(1)
        for m in range(2, pieces):
            t_rows_in(0, m)
        relay(1, 1, 1, 0)
        for m in range(2, pieces):
            t_plane(m).start()
        t_plane_in(1)
        relay(1, 1, 0, 0)
        send_own(0, 1, 1)
        send_own(0, 0, 1)
        if height > 4:
            relay(0, 1, 1, 0)
            relay(0, 1, 0, 0)
            relay_rest(0, 2)
        for m in range(2, pieces - 1):
            t_plane_in(m)
        t_rows_in(1, 0)
        relay(1, 0, 0, 1)
        relay(0, 0, 1, 1)
        relay(1, 0, 1, 1)
        t_rows_in(1, 1)
        t_plane_in(pieces - 1)
        relay(1, 1, 0, 1)
        for m in range(2, pieces - 1):
            t_rows_in(1, m)
        relay(0, 0, 0, 1)
        t_rows_in(1, pieces - 1)
        w_ready(0)
        wait_t_core(0)
        products(q, 0)
        relay(1, 1, 1, 1)
        if height > 4:
            relay(0, 1, 1, 1)
            relay(0, 1, 0, 1)
            relay_rest(1, 2)

        w_ready(1)
        products(q, 1)
        wait_t_core(1)
        products(1 - q, 1)
        products(1 - q, 0)
        finish_first()

    @pl.when(at_end)
    def _():
        t_plane_in(0)
        relay(0, 0, 0, 0)
        t_rows_in(0, 0)
        t_rows_in(0, 1)
        relay(0, 1, 0, 0)
        for m in range(2, pieces - 1):
            t_rows_in(0, m)
        t_plane_in(1)
        t_rows_in(0, pieces - 1)
        for step in range(2, height - 1):
            relay(0, step, 0, 0)
        t_rows_in(1, 0)
        for m in range(2, pieces - 1):
            t_plane_in(m)
        t_rows_in(1, 1)
        w_ready(0)
        wait_t_core(0)
        products(q, 0)
        t_plane_in(pieces - 1)
        for m in range(2, pieces - 1):
            t_rows_in(1, m)
        relay(0, 0, 0, 1)
        t_rows_in(1, pieces - 1)
        for step in range(1, height - 1):
            relay(0, step, 0, 1)
        wait_t_core(1)
        products(1 - q, 0)
        w_ready(1)
        products(q, 1)
        finish_first()
        products(1 - q, 1)

    for m in range(chunks):
        for block in range(height):
            for u in range(cuts):
                across(block, m, u).wait_send()
        for step in range(height - 1):
            for side in range(2):
                for kind in range(2):
                    @pl.when(sends(side, step, kind))
                    def _():
                        for u in range(cuts):
                            line_copy(side, step, kind, m, u).wait_send()
    for m in range(pieces):
        t_plane(m).wait_send()
        for k in range(2):
            for d in range(1, quads):
                t_row(k, d, m).wait_send()
            for d in range(quads):
                t_core(k, d, r, m).wait_send()

    if parts == 2:
        lax.fori_loop(1, 4, finish_next, 0)
    else:
        lax.fori_loop(0, chunks * occ, finish_whole, 0)

    def sent_mirror(n, carry):
        j, m = n // chunks, n % chunks
        for g in range(2):
            for py in range(2):
                @pl.when(jnp.logical_not(is_self(*mirror_peer_at(j, m, py))))
                def _():
                    mirror_copy(g, j, m, py).wait_send()
        return carry

    lax.fori_loop(0, chunks * occ, sent_mirror, 0)

    def last(n, carry):
        j = lax.rem(r + n, occ)
        place = lax.rem(n // occ + (jnp.where(inside, 1 - upper, upper) if parts == 2 else 0), chunks)
        update_copy(place, j).wait_recv()
        write(j, 1 - q, place, decoded(rin[place, j], scale))
        return carry

    lax.fori_loop(0, chunks * occ, last, 0)

    def sent_update(n, carry):
        update_copy(n // occ, n % occ).wait_send()
        return carry

    lax.fori_loop(0, chunks * occ, sent_update, 0)


def on_device(rows, cols, w_inter, t_panel, amplitudes, e_occ, e_vir):
    kw, occ_dev, vir_all = w_inter.shape
    vd, occ, kt = t_panel.shape
    height = cols // 2
    bound = LARGEST_T * LARGEST_W * kw * cols
    scale = 2.0 ** math.floor(119.0 / POWER - math.log2(bound))
    w_matrix = w_inter.reshape(kw, vir_all)
    half = vir_all // 2
    grouped = 2 if 2 * vd % 128 == 0 else 4
    width = grouped * vd
    chunks = half // width
    pairs = height // 4
    parts = 4 // grouped
    pieces = 4
    cuts = 2 if kw % 32 == 0 else 1
    dma = pltpu.SemaphoreType.DMA
    vmem = pl.BlockSpec(memory_space=pltpu.VMEM)
    hbm = pl.BlockSpec(memory_space=pltpu.HBM)
    lanes = max(128, vd)
    smem = pl.BlockSpec(memory_space=pltpu.SMEM)
    update = pl.pallas_call(
        functools.partial(kernel, rows, height, scale),
        out_shape=pltpu.VMEM((vd * occ * vir_all // lanes, lanes), jnp.float32),
        in_specs=[hbm, hbm, smem, vmem, vmem],
        out_specs=vmem,
        scratch_shapes=[
            pltpu.VMEM((vd, occ, kt), jnp.bfloat16),
            pltpu.VMEM((height, chunks, 2 * kw, width), jnp.bfloat16),
            pltpu.VMEM((height, chunks, kw, width), jnp.bfloat16),
            pltpu.VMEM((2, rows, occ * vd, kt), jnp.bfloat16),
            pltpu.VMEM((2, chunks, occ * vd, width), jnp.float32),
            pltpu.VMEM((2, occ, chunks, 2, grouped // 2, vd, vd), jnp.bfloat16),
            pltpu.VMEM((rows, pairs, 2, 2, parts, grouped // 2, vd, vd), jnp.bfloat16),
            pltpu.VMEM((chunks, occ, vd, width), jnp.bfloat16),
            pltpu.VMEM((chunks, occ, vd, width), jnp.bfloat16),
            dma((5,)),
            dma((chunks,)),
            dma((2, height - 1, 2, chunks, cuts)),
            dma((2, height - 1, 2, chunks, cuts)),
            dma((height, chunks, cuts)),
            dma((height, chunks, cuts)),
            dma((2, rows // 2, pieces)),
            dma((2, rows // 2, pieces)),
            dma((2, rows // 2, pieces)),
            dma((2, rows // 2, pieces)),
            dma((2, occ, chunks, 2)),
            dma((rows, pairs, 2, 2, parts)),
            dma((chunks, occ)),
            dma((chunks, occ)),
        ],
        compiler_params=pltpu.CompilerParams(
            collective_id=0, has_side_effects=True, vmem_limit_bytes=int(56 * 1024 * 1024)),
        name="amplitude_residual",
    )(w_matrix, t_panel, e_occ, e_vir.reshape(cols, vd), e_vir.reshape(vir_all // lanes, lanes))
    return (lax.optimization_barrier(amplitudes.reshape(update.shape)) + update).reshape(amplitudes.shape)


def solution(mesh):
    rows, cols = mesh.shape["row"], mesh.shape["col"]
    return jax.shard_map(
        functools.partial(on_device, rows, cols),
        mesh=mesh,
        in_specs=(
            P("col", "row", None),
            P("col", None, "row"),
            P("col", None, "row", None),
            P(),
            P(),
        ),
        out_specs=P("col", None, "row", None),
        check_vma=False,
    )
```
